512 devices in a mesh: ctx: 64 (over z, y), head: 8 (over x, core).
Axes of the slice: x: 4, y: 4, z: 16, core: 2. Of those that a mesh axis runs over, the one named last changes fastest.
Arguments:
- queries: bfloat16 [32768, 2048], P('ctx', 'head'), may hold values from -12 to 12
- keys: bfloat16 [32768, 2048], P('ctx', 'head'), may hold values from -12 to 12
- values: bfloat16 [32768, 4096], P('ctx', 'head'), may hold values from -6 to 6
- input_pre: float32 [32768, 8], P('ctx', 'head'), may hold values from -6 to 98
- forget_pre: float32 [32768, 8], P('ctx', 'head'), may hold values from -2 to 16
- output_pre: float32 [32768, 8], P('ctx', 'head'), may hold values from -8 to 8
- w_out: bfloat16 [4096, 4096], P('ctx', 'head'), may hold values from -0.25 to 0.25
Outputs:
- layer_out: bfloat16 [32768, 4096], P('ctx', 'head')
The draws below stay inside these ranges and needn't reach their ends.
All inputs are finite; a program needn't handle non-finite values.
Results may differ from the reference program's by a relative error of at most 0.0062.
Values may be sent and summed in bfloat16 or wider, within the bound.
A program may use at most 128 MiB of HBM per device.

```python
import jax
import jax.numpy as jnp
from jax import lax

DK = 256
DV = 512
TOK_DEV = 512
MEMORY_HEADS = 8
D = 4096
SEQUENCE_TOKENS = 32768
N_CTX = 64


def shared_signs(key):
    return jnp.where(jax.random.normal(jax.random.fold_in(key, 77), (MEMORY_HEADS * DK,)) > 0.0, 1.0, -1.0)


def quiet_heads(key):
    order = jax.random.permutation(jax.random.fold_in(key, 59), MEMORY_HEADS)
    return order < max(1, MEMORY_HEADS // 4)


def noisy_rows(key, salt):
    signs = shared_signs(key)
    inner = jax.random.fold_in(key, salt)
    noise = jnp.clip(jax.random.normal(inner, (SEQUENCE_TOKENS, MEMORY_HEADS * DK)), -4.0, 4.0)
    loud_cols = jnp.repeat(jnp.where(quiet_heads(key), 0.0, 1.0), DK)
    shift = 0.35 * signs * loud_cols
    return (noise + shift[None, :]).astype(jnp.bfloat16)


def draw_queries(key, part):
    return noisy_rows(key, 1)


def draw_keys(key, part):
    return noisy_rows(key, 2)


def draw_input_pre(key, part):
    inner = jax.random.fold_in(key, 31)
    base = jnp.clip(1.5 * jax.random.normal(inner, (SEQUENCE_TOKENS, MEMORY_HEADS)), -6.0, 6.0)
    level = jax.random.uniform(jax.random.fold_in(inner, 5), (MEMORY_HEADS,), minval=-5.5, maxval=-3.5)
    low = jnp.clip(level[None, :] + 0.5 * jax.random.normal(jax.random.fold_in(inner, 7), (SEQUENCE_TOKENS, MEMORY_HEADS)), -6.0, 6.0)
    return jnp.where(quiet_heads(key)[None, :], low, base)


def draw_forget_pre(key, part):
    base = jax.random.fold_in(key, 101)
    every_key_row = jax.random.split(base, 7)
    fast_share = 0.5
    is_fast = jax.random.uniform(every_key_row[0], (MEMORY_HEADS,)) < fast_share
    fast_rate = jnp.exp(jax.random.uniform(every_key_row[1], (MEMORY_HEADS,), minval=jnp.log(1.0 / 50.0), maxval=jnp.log(1.0 / 30.0)))
    slow_rate = jnp.exp(jax.random.uniform(every_key_row[2], (MEMORY_HEADS,), minval=jnp.log(0.1), maxval=jnp.log(0.8))) / SEQUENCE_TOKENS
    rate = jnp.where(is_fast, fast_rate, slow_rate)
    blocks = SEQUENCE_TOKENS // TOK_DEV
    block_factor = jnp.exp(jax.random.uniform(every_key_row[3], (blocks, 1, MEMORY_HEADS), minval=jnp.log(0.5), maxval=jnp.log(2.0)))
    token_factor = jax.random.uniform(every_key_row[4], (blocks, TOK_DEV, MEMORY_HEADS), minval=0.5, maxval=1.5)
    log_forget_gate = -(rate[None, None, :] * block_factor * token_factor).reshape(SEQUENCE_TOKENS, MEMORY_HEADS)
    spots = jax.random.randint(every_key_row[5], (3,), 0, SEQUENCE_TOKENS)
    masked_entries = jnp.any(jnp.arange(SEQUENCE_TOKENS)[:, None] == spots[None, :], axis=1)
    spike_penalty = jax.random.uniform(every_key_row[6], (SEQUENCE_TOKENS, MEMORY_HEADS), minval=0.22, maxval=0.51)
    log_forget_gate = log_forget_gate - jnp.where(masked_entries[:, None], spike_penalty, 0.0)
    return log_forget_gate - jnp.log(-jnp.expm1(log_forget_gate))


def spiked(entries, own_key, source, target, parts, factor):
    def block_of(axis_at):
        return (jnp.arange(entries.shape[axis_at]) // (entries.shape[axis_at] // parts)).reshape((-1,) + (1,) * (entries.ndim - 1 - axis_at))

    first = jax.random.permutation(own_key, parts)[block_of(target)]
    other_side = (block_of(target) + parts // 2) % parts
    return jnp.where((block_of(source) == first) | (block_of(source) == other_side), factor * entries, entries)


def level_of(stream_key, dims, shards, smallest, high):
    loudness = 1.0
    for axis_at, parts in shards:
        heights = jax.random.uniform(jax.random.fold_in(jax.random.fold_in(stream_key, 6), axis_at), (parts,), jnp.float32, smallest / len(shards), high / len(shards))
        loudness = loudness * jnp.repeat(jnp.exp(heights), dims[axis_at] // parts).reshape((-1,) + (1,) * (len(dims) - 1 - axis_at))
    return loudness


def scatter_about(key, extent, scale, limit, shards=(), dtype=jnp.bfloat16):
    factor_of = level_of(key, extent, shards, -0.22, 0.18) if shards else 1.0
    entries = jax.random.normal(key, extent, jnp.float32) * scale * factor_of
    return jnp.minimum(jnp.maximum(entries, -limit), limit).astype(dtype)


def bell_draw_with(key, extent, scale, bound, pieces, heavy, kind=jnp.bfloat16):
    values = scale * jax.random.normal(key, extent, jnp.float32)
    if pieces:
        values = values * level_of(key, extent, pieces, -0.22, 0.18)
    return jnp.clip(spiked(values, jax.random.fold_in(key, 3), *heavy), -bound, bound).astype(kind)


def setup_inputs(seed: int = 0) -> dict:
    key_list = jax.random.split(jax.random.key(seed), 8)
    return {
        "queries": draw_queries(jax.random.fold_in(key_list[7], 71), 0),
        "keys": draw_keys(jax.random.fold_in(key_list[7], 71), 0),
        "values": scatter_about(key_list[2], (SEQUENCE_TOKENS, MEMORY_HEADS * DV), 1.0, 6.0, ((0, 64), (1, 8))),
        "input_pre": draw_input_pre(jax.random.fold_in(key_list[7], 71), 0),
        "forget_pre": draw_forget_pre(jax.random.fold_in(key_list[7], 71), 0),
        "output_pre": scatter_about(key_list[5], (SEQUENCE_TOKENS, MEMORY_HEADS), 1.5, 8.0, ((0, 64), (1, 8)), jnp.float32),
        "w_out": bell_draw_with(key_list[6], (D, D), D ** -0.5, 0.25, ((0, 64), (1, 8)), (0, 1, 64, 4.0)),
    }


def combine(earlier, later):
    mem_a, norm_a, top_a, decay_a = earlier
    mem_b, norm_b, top_b, decay_b = later
    top_log = jnp.maximum(decay_b + top_a, top_b)
    keep_old = jnp.exp(decay_b + top_a - top_log)
    fresh_w = jnp.exp(top_b - top_log)
    return (keep_old * mem_a + fresh_w * mem_b, keep_old * norm_a + fresh_w * norm_b, top_log, decay_a + decay_b)


def block_pass(query_b, key_b, value_b, forget_b, input_b, outgate_b, carried):
    memory, norm_vec, top_prev = carried
    tok_rows = query_b.shape[0]
    score_scale = DK ** -0.5
    log_forget_gate = jax.nn.log_sigmoid(forget_b)
    cum_decay = jnp.cumsum(log_forget_gate)
    block_decay = cum_decay[-1]
    rest_gain = block_decay - cum_decay + input_b
    top_local = jnp.max(rest_gain)
    key_weight = jnp.exp(rest_gain - top_local)
    scaled = key_b.astype(jnp.float32) * key_weight[:, None]
    memory_local = jnp.dot(scaled.astype(jnp.bfloat16).T, value_b, preferred_element_type=jnp.float32)
    norm_local = jnp.sum(scaled, axis=0)
    scores = jnp.dot(query_b, key_b.T, preferred_element_type=jnp.float32) * score_scale
    causal = jnp.arange(tok_rows)[:, None] >= jnp.arange(tok_rows)[None, :]
    rel_gain = jnp.where(causal, cum_decay[:, None] - cum_decay[None, :] + input_b[None, :], -1e30)
    top_tok = jnp.maximum(cum_decay + top_prev, jnp.max(rel_gain, axis=1))
    weighted = jnp.exp(rel_gain - top_tok[:, None]) * scores
    den_in = jnp.sum(weighted, axis=1)
    numerator_input = jnp.dot(weighted.astype(jnp.bfloat16), value_b, preferred_element_type=jnp.float32)
    lift = jnp.exp(cum_decay + top_prev - top_tok)
    num_out = jnp.dot(query_b, memory.astype(jnp.bfloat16), preferred_element_type=jnp.float32) * score_scale
    normalizer_output = jnp.dot(query_b.astype(jnp.float32), norm_vec, precision=lax.Precision.HIGHEST) * score_scale
    numer = numerator_input + lift[:, None] * num_out
    denom = jnp.maximum(jnp.abs(den_in + lift * normalizer_output), jnp.exp(-top_tok))
    hidden = numer / denom[:, None]
    gated_out = (jax.nn.sigmoid(outgate_b)[:, None] * hidden).astype(jnp.bfloat16)
    state_next = combine((memory, norm_vec, top_prev, jnp.zeros((), jnp.float32)), (memory_local, norm_local, top_local, block_decay))
    return state_next[:3], gated_out


def one_head(inputs):
    query_h, key_h, value_h, forget_h, input_h, outgate_h = inputs
    start_state = (jnp.zeros((DK, DV), jnp.float32), jnp.zeros((DK,), jnp.float32), jnp.array(-1e30, jnp.float32))

    def advance(carried, block_in):
        return block_pass(*block_in, carried)

    _, outputs = lax.scan(advance, start_state, (query_h, key_h, value_h, forget_h, input_h, outgate_h))
    return outputs


def split_heads(array, width):
    return array.reshape(SEQUENCE_TOKENS, MEMORY_HEADS, width).transpose(1, 0, 2).reshape(MEMORY_HEADS, N_CTX, TOK_DEV, width)


def split_gates(array):
    return array.T.reshape(MEMORY_HEADS, N_CTX, TOK_DEV)


def reference(queries, keys, values, input_pre, forget_pre, output_pre, w_out):
    gated_heads = lax.map(one_head, (split_heads(queries, DK), split_heads(keys, DK), split_heads(values, DV), split_gates(forget_pre), split_gates(input_pre), split_gates(output_pre)))
    gated_all = gated_heads.reshape(MEMORY_HEADS, SEQUENCE_TOKENS, DV).transpose(1, 0, 2).reshape(SEQUENCE_TOKENS, D)
    return jnp.dot(gated_all, w_out, preferred_element_type=jnp.float32).astype(jnp.bfloat16)
```

```python
import functools

import jax
import jax.numpy as jnp
from jax import lax
from jax.experimental import pallas as pl
from jax.experimental.pallas import tpu as pltpu
from jax.sharding import PartitionSpec as P

MESH = pl.DeviceIdType.MESH
F32 = jnp.float32
BF16 = jnp.bfloat16
NY = 4
CHUNKS = 4


def _log_sigmoid(f):
    e = jnp.exp(-jnp.abs(f))
    s = e / (2.0 + e)
    s2 = s * s
    poly = jnp.full_like(s, 1.0 / 15.0)
    for d in (13.0, 11.0, 9.0, 7.0, 5.0, 3.0, 1.0):
        poly = poly * s2 + 1.0 / d
    return jnp.minimum(f, 0.0) - 2.0 * s * poly


def _combine_top(top, decay, fresh):
    new = jnp.maximum(decay + top, fresh)
    return new, jnp.exp(decay + top - new), jnp.exp(fresh - new)


def _wide(row, n):
    return jnp.concatenate([row] * n, axis=1)


def kernel(nz, ny, nx, q_ref, k_ref, v_ref, i_ref, f_ref, o_ref, w_ref, out_ref, *scr):
    (mloc, ybuf, sy, tt, stt, ta, sta, pb, sp, pz, mo, sm, mem, gbuf, wbuf, base, gbc, cols,
     s1s, s1r, s1bs, s1br, s3s, s3r, s3bs, s3br, s5s, s5r, s6s, s6r,
     wfs, wfr, wbs, wbr, yps, ypr, yms, ymr, y2s, y2r, xs, xr, bs, br) = scr
    tok, dk = q_ref.shape
    dv = v_ref.shape[1]
    wr = w_ref.shape[0]
    nh = 2 * nx
    qr = dk // ny
    lt = dv // 128
    nt = (qr // 16) * lt
    tpo = nt // nz
    scale = dk ** (-0.5)
    c = lax.axis_index("ctx")
    h = lax.axis_index("head")
    z, y = lax.div(c, ny), lax.rem(c, ny)
    x, core = lax.div(h, 2), lax.rem(h, 2)
    sib = h + 1 - 2 * core

    def zat(d):
        return lax.rem(z + (d + nz), nz)

    def yat(d):
        return lax.rem(y + (d + ny), ny)

    def hat(d):
        return lax.rem(x + (d + nx), nx) * 2 + core

    def dev(zz, yy, hh):
        return (zz * ny + yy, hh)

    def rcopy(src, dst, ss, rs, to):
        return pltpu.make_async_remote_copy(
            src_ref=src, dst_ref=dst, send_sem=ss, recv_sem=rs, device_id=to, device_id_type=MESH
        )

    partners = [dev(z, yat(d), h) for d in range(1, ny)]
    partners += [dev(zat(d), y, h) for d in range(1, nz)]
    if nx > 1:
        partners += [(c, hat(1)), (c, hat(-1))]
    partners += [(c, sib)]
    barrier = pltpu.get_barrier_semaphore()
    for p in partners:
        pl.semaphore_signal(barrier, inc=1, device_id=p, device_id_type=MESH)

    def wpiece(dz, dy):
        row = pl.multiple_of((zat(dz) * ny + yat(dy)) * wr, wr)
        return wbuf.at[pl.ds(row, wr), :]

    nf = nz // 2
    nb = nz - 1 - nf

    def wz(step, sign):
        src = w_ref if step == 1 else wpiece(-sign * (step - 1), 0)
        dst = wpiece(-sign * (step - 1), 0)
        ss, rs = (wfs, wfr) if sign > 0 else (wbs, wbr)
        return rcopy(src, dst, ss.at[step - 1], rs.at[step - 1], dev(zat(sign), y, h))

    def wz_got(step, sign):
        ss, rs = (wfs, wfr) if sign > 0 else (wbs, wbr)
        piece = wpiece(-sign * step, 0)
        return rcopy(piece, piece, ss.at[step - 1], rs.at[step - 1], dev(zat(sign), y, h))

    def wy(j, sign):
        src = w_ref if j == 0 else wpiece(j, 0)
        ss, rs = (yps, ypr) if sign > 0 else (yms, ymr)
        return rcopy(src, wpiece(j, 0), ss.at[j + nf], rs.at[j + nf], dev(z, yat(sign), h))

    def wy_got(j, sign):
        piece = wpiece(j, -sign)
        ss, rs = (yps, ypr) if sign > 0 else (yms, ymr)
        return rcopy(piece, piece, ss.at[j + nf], rs.at[j + nf], dev(z, yat(sign), h))

    def wy2(j):
        sign = 1 if j % 2 == 0 else -1
        piece = wpiece(j, -sign)
        return rcopy(piece, piece, y2s.at[j + nf], y2r.at[j + nf], dev(z, yat(sign), h))

    def wy2_got(j):
        sign = 1 if j % 2 == 0 else -1
        piece = wpiece(j, -2 * sign)
        return rcopy(piece, piece, y2s.at[j + nf], y2r.at[j + nf], dev(z, yat(sign), h))

    rels = list(range(-nf, nb + 1))

    def w_step(step):
        for sign, last in ((1, nf), (-1, nb)):
            if step <= last:
                wz_got(step, sign).wait_recv()
                if step + 1 <= last:
                    wz(step + 1, sign).start()

    def w_across(js):
        if ny > 1:
            for j in js:
                wy(j, 1).start()
                wy(j, -1).start()

    def w_relay(js):
        if ny > 1:
            for j in js:
                for sign in (1, -1):
                    wy_got(j, sign).wait_recv()
                wy2(j).start()

    lane = lax.broadcasted_iota(jnp.int32, (8, tok), 1)
    gate_in = jnp.broadcast_to(i_ref[...], (8, tok))
    cum = _log_sigmoid(jnp.broadcast_to(f_ref[...], (8, tok)))
    sh = 1
    while sh < tok:
        cum = cum + jnp.where(lane >= sh, pltpu.roll(cum, sh, 1), 0.0)
        sh *= 2
    a_row = gate_in - cum
    top_row = a_row
    sh = 1
    while sh < tok:
        top_row = jnp.maximum(top_row, jnp.where(lane >= sh, pltpu.roll(top_row, sh, 1), -3e38))
        sh *= 2
    sig = 1.0 / (1.0 + jnp.exp(-jnp.broadcast_to(o_ref[...], (8, tok))))
    decay = cum[0:1, tok - 1:tok]
    a_last = top_row[0:1, tok - 1:tok]
    kw_row = jnp.exp(a_row - a_last)
    rows = lax.broadcasted_iota(jnp.int32, (128, tok), 0)
    stack = jnp.where(rows == 0, top_row[0:1], jnp.where(rows == 1, cum[0:1],
            jnp.where(rows == 2, sig[0:1], kw_row[0:1])))
    cols[...] = jnp.transpose(stack)
    a1 = a_row[0:1]

    scaled = k_ref[...].astype(F32) * cols[:, 3:4]
    norm = jnp.sum(scaled, axis=0, keepdims=True)
    m_local = lax.dot_general(
        scaled.astype(BF16), v_ref[...], (((0,), (0,)), ((), ())), preferred_element_type=F32
    )
    for j in range(ny):
        mloc[j] = m_local[j * qr:(j + 1) * qr].astype(BF16)
    pad = [jnp.zeros((4, 128), F32)]
    stat = jnp.concatenate(
        [norm[:, 0:128], norm[:, 128:256], jnp.broadcast_to(decay, (1, 128)),
         jnp.broadcast_to(decay + a_last, (1, 128))] + pad, axis=0)
    sy[y] = stat
    ybuf[y] = mloc[y]
    own_rows = pl.multiple_of(c * wr, wr)
    wbuf[pl.ds(own_rows, wr), :] = w_ref[...]

    pl.semaphore_wait(barrier, len(partners))

    def s1(d):
        return rcopy(mloc.at[yat(d)], ybuf.at[y], s1s.at[d - 1], s1r.at[d - 1], dev(z, yat(d), h))

    def s1b(d):
        return rcopy(sy.at[y], sy.at[y], s1bs.at[d - 1], s1br.at[d - 1], dev(z, yat(d), h))

    def s1_got(d):
        return rcopy(mloc.at[y], ybuf.at[yat(-d)], s1s.at[d - 1], s1r.at[d - 1], dev(z, yat(d), h))

    def s1b_got(d):
        return rcopy(sy.at[y], sy.at[yat(-d)], s1bs.at[d - 1], s1br.at[d - 1], dev(z, yat(d), h))

    for d in range(1, ny):
        s1b(d).start()
        s1(d).start()
    if nf:
        wz(1, 1).start()
    if nb:
        wz(1, -1).start()

    rb = 128
    dens = []
    for r in range(tok // rb):
        width = (r + 1) * rb
        sl = pl.ds(r * rb, rb)
        scores = lax.dot_general(
            q_ref[sl, :], k_ref[0:width, :], (((1,), (1,)), ((), ())), preferred_element_type=F32
        ) * scale
        ti = lax.broadcasted_iota(jnp.int32, (rb, width), 0) + r * rb
        si = lax.broadcasted_iota(jnp.int32, (rb, width), 1)
        rel = jnp.where(ti >= si, a1[:, 0:width] - cols[sl, 0:1], -1e30)
        weighted = jnp.exp(rel) * scores
        dens.append(jnp.sum(weighted, axis=1, keepdims=True))
        base[sl, :] = jnp.dot(weighted.astype(BF16), v_ref[0:width, :], preferred_element_type=F32)
    den_loc = jnp.concatenate(dens, axis=0)

    w_step(1)

    for d in range(1, ny):
        s1b_got(d).wait_recv()
        s1_got(d).wait_recv()
    dec = [sy[j, 2:3, :] for j in range(ny)]
    tops = [sy[j, 3:4, :] for j in range(ny)]
    suffix = jnp.zeros((1, 128), F32)
    logs = [None] * ny
    for j in reversed(range(ny)):
        logs[j] = suffix + tops[j]
        suffix = suffix + dec[j]
    top_t = functools.reduce(jnp.maximum, logs)
    wts = [jnp.exp(lg - top_t) for lg in logs]
    total = sum(_wide(wts[j], lt) * ybuf[j].astype(F32) for j in range(ny))
    for t in range(nt):
        a, b = divmod(t, lt)
        o, s = divmod(t, tpo)
        tt[o, s * 16:(s + 1) * 16, :] = total[a * 16:(a + 1) * 16, b * 128:(b + 1) * 128].astype(BF16)
    norm_t = sum(wts[j] * sy[j, 0:2, :] for j in range(ny))
    stt[...] = jnp.concatenate([norm_t, suffix, top_t] + pad, axis=0)
    ta[z] = tt[z]
    sta[z] = stt[...]

    def s3(d):
        return rcopy(tt.at[zat(d)], ta.at[z], s3s.at[d - 1], s3r.at[d - 1], dev(zat(d), y, h))

    def s3b(d):
        return rcopy(stt, sta.at[z], s3bs.at[d - 1], s3br.at[d - 1], dev(zat(d), y, h))

    def s3_got(d):
        return rcopy(tt.at[z], ta.at[zat(-d)], s3s.at[d - 1], s3r.at[d - 1], dev(zat(d), y, h))

    def s3b_got(d):
        return rcopy(stt, sta.at[zat(-d)], s3bs.at[d - 1], s3br.at[d - 1], dev(zat(d), y, h))

    far = sorted(range(1, nz), key=lambda d: -min(d, nz - d))
    for d in far:
        s3b(d).start()
        s3(d).start()

    w_across([0])
    w_step(2)
    w_across([j for j in (-1, 1) if j in rels])
    w_step(3)
    w_across([j for j in (-2, 2) if j in rels])
    w_step(4)

    for d in far:
        s3b_got(d).wait_recv()
        s3_got(d).wait_recv()
    state = jnp.zeros((tpo * 16, 128), F32)
    norm_p = jnp.zeros((2, 128), F32)
    top_p = jnp.full((1, 128), -1e30, F32)
    for zz in range(nz):
        pb[zz] = state.astype(BF16)
        sp[zz, 0:2, :] = norm_p
        sp[zz, 2:3, :] = top_p
        if zz + 1 < nz:
            top_p, keep, fresh = _combine_top(top_p, sta[zz, 2:3, :], sta[zz, 3:4, :])
            state = keep * state + fresh * ta[zz].astype(F32)
            norm_p = keep * norm_p + fresh * sta[zz, 0:2, :]
    pz[z] = pb[z]

    def s5(d):
        return rcopy(pb.at[zat(d)], pz.at[z], s5s.at[d - 1], s5r.at[d - 1], dev(zat(d), y, h))

    def s5_got(d):
        return rcopy(pb.at[z], pz.at[zat(-d)], s5s.at[d - 1], s5r.at[d - 1], dev(zat(d), y, h))

    for d in far:
        s5(d).start()

    norm_p = sp[z, 0:2, :]
    top_p = sp[z, 2:3, :]
    keeps, freshs = [], []
    for j in range(ny):
        sm[j, 0:2, :] = norm_p
        sm[j, 2:3, :] = top_p
        if j + 1 < ny:
            top_p, keep, fresh = _combine_top(top_p, dec[j], tops[j])
            keeps.append(keep)
            freshs.append(fresh)
            norm_p = keep * norm_p + fresh * sy[j, 0:2, :]
    norm_prev = sm[y, 0:2, :]
    top_prev = sm[y, 2:3, :][:, 0:1]
    norm_row = jnp.concatenate([norm_prev[0:1], norm_prev[1:2]], axis=1)
    q_norm = jnp.sum(q_ref[...].astype(F32) * norm_row, axis=1, keepdims=True) * scale
    top_loc = cols[:, 0:1]
    top_mix = jnp.maximum(top_loc, top_prev)
    inner = jnp.exp(top_loc - top_mix)
    lift = jnp.exp(top_prev - top_mix)
    den = jnp.maximum(
        jnp.abs(inner * den_loc + lift * q_norm), jnp.exp(-(cols[:, 1:2] + top_mix)))
    gate = cols[:, 2:3] / den
    base[...] = base[...] * (gate * inner)
    gbc[...] = jnp.broadcast_to(gate * lift * scale, gbc.shape)

    w_across([j for j in (-3, 3) if j in rels])
    w_step(5)
    w_relay([0])
    w_step(6)

    for d in far:
        s5_got(d).wait_recv()
    tiles = [pz[t // tpo, (t % tpo) * 16:(t % tpo + 1) * 16, :].astype(F32) for t in range(nt)]
    state = jnp.concatenate(
        [jnp.concatenate(tiles[a * lt:(a + 1) * lt], axis=1) for a in range(qr // 16)], axis=0)
    for j in range(ny):
        mo[j] = state.astype(BF16)
        if j + 1 < ny:
            state = _wide(keeps[j], lt) * state + _wide(freshs[j], lt) * ybuf[j].astype(F32)
    mem[pl.ds(pl.multiple_of(y * qr, qr), qr), :] = mo[y]

    def s6(d):
        return rcopy(mo.at[yat(d)], mem.at[pl.ds(pl.multiple_of(y * qr, qr), qr), :],
                     s6s.at[d - 1], s6r.at[d - 1], dev(z, yat(d), h))

    def s6_got(d):
        return rcopy(mo.at[y], mem.at[pl.ds(pl.multiple_of(yat(-d) * qr, qr), qr), :],
                     s6s.at[d - 1], s6r.at[d - 1], dev(z, yat(d), h))

    for d in range(1, ny):
        s6(d).start()
    w_step(7)
    w_across([j for j in (-4, -5, 4, 5) if j in rels])
    w_relay([j for j in (-1, 1, -2, 2) if j in rels])
    for d in range(1, ny):
        s6_got(d).wait_recv()

    cr = tok // CHUNKS

    def gchunk(hh, r):
        return gbuf.at[hh, pl.ds(r * cr, cr), :]

    def xcopy(slot, hh, r, to):
        piece = gchunk(hh, r)
        return rcopy(piece, piece, xs.at[slot, r], xr.at[slot, r], to)

    def scopy(slot, hh, r):
        piece = gchunk(hh, r)
        return rcopy(piece, piece, bs.at[slot, r], br.at[slot, r], (c, sib))

    for r in range(CHUNKS):
        sl = pl.ds(r * cr, cr)
        out = jnp.dot(q_ref[sl, :], mem[...], preferred_element_type=F32)
        gbuf[h, sl, :] = (base[sl, :] + _wide(gbc[sl, :], lt) * out).astype(BF16)
        if nx > 1:
            xcopy(0, h, r, (c, hat(1))).start()
            xcopy(1, h, r, (c, hat(-1))).start()
        scopy(0, h, r).start()

    half = CHUNKS // 2
    rest = [j for j in (-6, 6, -7, 7, -8) if j in rels]
    w_step(8)
    w_across(rest)
    if nx > 1:
        for r in range(CHUNKS):
            xcopy(0, hat(-1), r, (c, hat(1))).wait_recv()
            if r < half:
                xcopy(2, hat(-1), r, (c, hat(1))).start()
            scopy(1, hat(-1), r).start()
            xcopy(1, hat(1), r, (c, hat(-1))).wait_recv()
            if r >= half:
                xcopy(2, hat(1), r, (c, hat(-1))).start()
            scopy(2, hat(1), r).start()
            w_relay([j for j in ((-3, 3), (-4, 4), (-5, 5), (-6, 6))[r] if j in rels])
        for r in range(CHUNKS):
            xcopy(2, hat(2), r, (c, hat(1))).wait_recv()
            scopy(3, hat(2), r).start()
    else:
        w_relay([j for j in (-3, 3, -4, 4, -5, 5, -6, 6) if j in rels])
    w_relay([j for j in (-7, 7, -8) if j in rels])
    if ny > 1:
        for j in rels:
            wy2_got(j).wait_recv()
    sib_x = lax.div(sib, 2) * 2 + 1 - core

    def hat_sib(d):
        return lax.rem(x + (d + nx), nx) * 2 + 1 - core

    for r in range(CHUNKS):
        scopy(0, sib_x, r).wait_recv()
        if nx > 1:
            scopy(1, hat_sib(-1), r).wait_recv()
            scopy(2, hat_sib(1), r).wait_recv()
            scopy(3, hat_sib(2), r).wait_recv()

    for rr in range(tok // 256):
        for cc in range(dv // 256):
            acc = jnp.zeros((256, 256), F32)
            for hh in range(nh):
                acc = acc + jnp.dot(
                    gbuf[hh, rr * 256:(rr + 1) * 256, :],
                    wbuf[hh * dv:(hh + 1) * dv, cc * 256:(cc + 1) * 256],
                    preferred_element_type=F32)
            out_ref[rr * 256:(rr + 1) * 256, cc * 256:(cc + 1) * 256] = acc.astype(BF16)

    for d in range(1, ny):
        s1(d).wait_send()
        s1b(d).wait_send()
        s6(d).wait_send()
    for d in range(1, nz):
        s3(d).wait_send()
        s3b(d).wait_send()
        s5(d).wait_send()
    for sign, last in ((1, nf), (-1, nb)):
        for step in range(1, last + 1):
            wz(step, sign).wait_send()
    if ny > 1:
        for j in rels:
            wy(j, 1).wait_send()
            wy(j, -1).wait_send()
            wy2(j).wait_send()
    for r in range(CHUNKS):
        scopy(0, h, r).wait_send()
        if nx > 1:
            xcopy(0, h, r, (c, hat(1))).wait_send()
            xcopy(1, h, r, (c, hat(-1))).wait_send()
            if r < half:
                xcopy(2, hat(-1), r, (c, hat(1))).wait_send()
            else:
                xcopy(2, hat(1), r, (c, hat(-1))).wait_send()
            scopy(1, hat(-1), r).wait_send()
            scopy(2, hat(1), r).wait_send()
            scopy(3, hat(2), r).wait_send()


def local(nz, ny, nx, queries, keys, values, input_pre, forget_pre, output_pre, w_out):
    tok, dk = queries.shape
    dv = values.shape[1]
    nh = 2 * nx
    qr = dk // ny
    tpo = (qr // 16) * (dv // 128) // nz
    dma = pltpu.SemaphoreType.DMA
    v = pltpu.VMEM
    y1, z1 = max(ny - 1, 1), max(nz - 1, 1)
    scratch = [
        v((ny, qr, dv), BF16), v((ny, qr, dv), BF16), v((ny, 8, 128), F32),
        v((nz, tpo * 16, 128), BF16), v((8, 128), F32),
        v((nz, tpo * 16, 128), BF16), v((nz, 8, 128), F32),
        v((nz, tpo * 16, 128), BF16), v((nz, 8, 128), F32),
        v((nz, tpo * 16, 128), BF16), v((ny, qr, dv), BF16), v((ny, 8, 128), F32),
        v((dk, dv), BF16), v((nh, tok, dv), BF16), v((nh * dv, dv), BF16),
        v((tok, dv), F32), v((tok, 128), F32), v((tok, 128), F32),
        dma((y1,)), dma((y1,)), dma((y1,)), dma((y1,)),
        dma((z1,)), dma((z1,)), dma((z1,)), dma((z1,)), dma((z1,)), dma((z1,)),
        dma((y1,)), dma((y1,)),
        dma((nz,)), dma((nz,)), dma((nz,)), dma((nz,)),
        dma((nz,)), dma((nz,)), dma((nz,)), dma((nz,)), dma((nz,)), dma((nz,)),
        dma((3, CHUNKS)), dma((3, CHUNKS)), dma((4, CHUNKS)), dma((4, CHUNKS)),
    ]
    return pl.pallas_call(
        functools.partial(kernel, nz, ny, nx),
        out_shape=jax.ShapeDtypeStruct((tok, dv), BF16),
        in_specs=[pl.BlockSpec(memory_space=pltpu.VMEM)] * 7,
        out_specs=pl.BlockSpec(memory_space=pltpu.VMEM),
        scratch_shapes=scratch,
        compiler_params=pltpu.CompilerParams(
            collective_id=0, has_side_effects=True, vmem_limit_bytes=48 * 1024 * 1024),
        name="mlstm_layer",
    )(queries, keys, values, input_pre.reshape(1, tok), forget_pre.reshape(1, tok),
      output_pre.reshape(1, tok), w_out)


def solution(mesh, ny=NY):
    nz = mesh.shape["ctx"] // ny
    nx = mesh.shape["head"] // 2
    spec = P("ctx", "head")
    return jax.shard_map(
        functools.partial(local, nz, ny, nx), mesh=mesh, in_specs=(spec,) * 7, out_specs=spec,
        check_vma=False)
```

```python
import functools

import jax
import jax.numpy as jnp
from jax import lax
from jax.experimental import pallas as pl
from jax.experimental.pallas import tpu as pltpu
from jax.sharding import PartitionSpec as P

MESH = pl.DeviceIdType.MESH
F32 = jnp.float32
BF16 = jnp.bfloat16
NY = 4


def _log_sigmoid(f):
    e = jnp.exp(-jnp.abs(f))
    s = e / (2.0 + e)
    s2 = s * s
    poly = jnp.full_like(s, 1.0 / 15.0)
    for d in (13.0, 11.0, 9.0, 7.0, 5.0, 3.0, 1.0):
        poly = poly * s2 + 1.0 / d
    return jnp.minimum(f, 0.0) - 2.0 * s * poly


def _combine_top(top, decay, fresh):
    new = jnp.maximum(decay + top, fresh)
    return new, jnp.exp(decay + top - new), jnp.exp(fresh - new)


def _wide(row, n):
    return jnp.concatenate([row] * n, axis=1)


class Sems:
    def __init__(self, name, ref):
        self.name, self.ref = name, ref

    def __call__(self, *index):
        return (self.name,) + index, self.ref.at[index if len(index) > 1 else index[0]]


def kernel(nz, ny, nx, q_hbm, k_hbm, v_hbm, i_hbm, f_hbm, o_hbm, w_hbm, out_ref, *scr):
    (k_ref, v_ref, i_ref, f_ref, o_ref, ins, mloc, ybuf, sy, tt, stt, ta, sta, pb, sp, pz, mo, sm, cols,
     qbuf, nbuf, mbuf, cbuf, gbuf, wa, wb, *sems) = scr
    (s1s, s1r, s1bs, s1br, s3s, s3r, s3bs, s3br, s5s, s5r, s6s, s6r, wafs, wafr, wabs, wabr,
     wbfs, wbfr, wbbs, wbbr, w0s, w0r, yps, ypr, yms, ymr, y2s, y2r, xs, xr, bs, br, cs, cr) = [
        Sems(n, ref) for n, ref in enumerate(sems)]
    tok, dk = k_ref.shape
    dv = v_ref.shape[1]
    wr = w_hbm.shape[0]
    wc = dv // 2
    nh = 2 * nx
    qr = dk // ny
    lt = dv // 128
    nt = (qr // 16) * lt
    tpo = nt // nz
    scale = dk ** (-0.5)
    c = lax.axis_index("ctx")
    h = lax.axis_index("head")
    z, y = lax.div(c, ny), lax.rem(c, ny)
    x, core = lax.div(h, 2), lax.rem(h, 2)
    sib = h + 1 - 2 * core

    def wpiece(buf, dz, dy):
        row = pl.multiple_of((zat(dz) * ny + yat(dy)) * wr, wr)
        return buf.at[pl.ds(row, wr), :]

    def zat(d):
        return lax.rem(z + (d + nz), nz)

    def yat(d):
        return lax.rem(y + (d + ny), ny)

    def hat(d, other=0):
        side = 1 - core if other else core
        return lax.rem(x + (d + nx), nx) * 2 + side

    def dev(zz, yy, hh):
        return (zz * ny + yy, hh)

    loads = [
        pltpu.make_async_copy(src, dst, ins.at[n]) for n, (src, dst) in enumerate((
            (f_hbm, f_ref), (i_hbm, i_ref), (o_hbm, o_ref), (k_hbm, k_ref), (v_hbm, v_ref),
            (q_hbm, qbuf.at[h]),
            (w_hbm.at[:, 0:wc], wpiece(wa, 0, 0)), (w_hbm.at[:, wc:dv], wpiece(wb, 0, 0))))
    ]
    for load in loads:
        load.start()

    started, got = {}, set()

    def send(src, dst, ss, rs, to):
        copy = pltpu.make_async_remote_copy(
            src_ref=src, dst_ref=dst, send_sem=ss[1], recv_sem=rs[1], device_id=to, device_id_type=MESH)
        started[rs[0]] = copy
        copy.start()

    def take(rs):
        got.add(rs[0])
        started[rs[0]].wait_recv()

    partners = [dev(z, yat(d), h) for d in range(1, ny)]
    partners += [dev(zat(d), y, h) for d in range(1, nz)]
    partners += [(c, lax.rem(h + d, nh)) for d in range(1, nh)]
    barrier = pltpu.get_barrier_semaphore()
    for p in partners:
        pl.semaphore_signal(barrier, inc=1, device_id=p, device_id_type=MESH)

    nf = nz // 2
    nb = nz - 1 - nf
    rels = list(range(-nf, nb + 1))
    half_plane = ny * wr // 2

    def plane(dz, part):
        row = pl.multiple_of(zat(dz) * (ny * wr) + part * half_plane, half_plane)
        return wb.at[pl.ds(row, half_plane), :]

    def wa_send(step, sign):
        piece = wpiece(wa, -sign * (step - 1), 0)
        ss, rs = (wafs, wafr) if sign > 0 else (wabs, wabr)
        send(piece, piece, ss(step - 1), rs(step - 1), dev(zat(sign), y, h))

    def wb_send(step, sign, part):
        piece = plane(-sign * (step - 1), part)
        ss, rs = (wbfs, wbfr) if sign > 0 else (wbbs, wbbr)
        send(piece, piece, ss(step - 1, part), rs(step - 1, part), dev(zat(sign), y, h))

    ways = ((1, nf, wafr, wbfr), (-1, nb, wabr, wbbr))

    def wa_step(step):
        for sign, last, ra, _ in ways:
            if 1 <= step <= last:
                take(ra(step - 1))
            if step + 1 <= last:
                wa_send(step + 1, sign)

    def wb_step(step):
        for part in (0, 1):
            for sign, last, _, rb in ways:
                if 1 <= step <= last:
                    take(rb(step - 1, part))
                if step + 1 <= last:
                    wb_send(step + 1, sign, part)

    def wb_first():
        for d in range(1, ny):
            piece = wpiece(wb, 0, 0)
            send(piece, piece, w0s(d - 1), w0r(d - 1), dev(z, yat(d), h))

    def wb_row():
        for d in range(1, ny):
            take(w0r(d - 1))
        wb_step(0)

    def wa_across(*js):
        for j in js:
            if ny > 1 and j in rels:
                piece = wpiece(wa, j, 0)
                send(piece, piece, yps(j + nf), ypr(j + nf), dev(z, yat(1), h))
                send(piece, piece, yms(j + nf), ymr(j + nf), dev(z, yat(-1), h))

    def wa_relay(*js):
        for j in js:
            if ny > 1 and j in rels:
                take(ypr(j + nf))
                take(ymr(j + nf))
                sign = 1 if j % 2 == 0 else -1
                piece = wpiece(wa, j, -sign)
                send(piece, piece, y2s(j + nf), y2r(j + nf), dev(z, yat(sign), h))

    def item(n, hh):
        if n < 2:
            return qbuf.at[hh, pl.ds(n * (tok // 2), tok // 2), :]
        if n < 6:
            return nbuf.at[hh, pl.ds((n - 2) * (tok // 4), tok // 4), :]
        return mbuf.at[hh, pl.ds(pl.multiple_of(yat(6 - n) * qr, qr), qr), :]

    def onward(n):
        return 1 if n in (0, 2, 3, 6, 7) else -1

    def x_side(n, slot, hh):
        piece = item(n, hh)
        send(piece, piece, bs(slot, n), br(slot, n), (c, sib))

    def x_send(n):
        piece = item(n, h)
        if nx > 1:
            send(piece, piece, xs(0, n), xr(0, n), (c, hat(1)))
            send(piece, piece, xs(1, n), xr(1, n), (c, hat(-1)))
        x_side(n, 0, h)

    def x_relay(n):
        if nx > 1:
            for slot, d in ((0, -1), (1, 1)):
                take(xr(slot, n))
                if onward(n) == -d:
                    piece = item(n, hat(d))
                    send(piece, piece, xs(2, n), xr(2, n), (c, hat(-d)))
                x_side(n, 1 + slot, hat(d))

    def x_last(n):
        if nx > 1:
            take(xr(2, n))
            x_side(n, 3, hat(2))

    for load in loads[0:3]:
        load.wait()
    lane = lax.broadcasted_iota(jnp.int32, (8, tok), 1)
    gate_in = jnp.broadcast_to(i_ref[...], (8, tok))
    cum = _log_sigmoid(jnp.broadcast_to(f_ref[...], (8, tok)))
    sh = 1
    while sh < tok:
        cum = cum + jnp.where(lane >= sh, pltpu.roll(cum, sh, 1), 0.0)
        sh *= 2
    a_row = gate_in - cum
    top_row = a_row
    sh = 1
    while sh < tok:
        top_row = jnp.maximum(top_row, jnp.where(lane >= sh, pltpu.roll(top_row, sh, 1), -3e38))
        sh *= 2
    sig = 1.0 / (1.0 + jnp.exp(-jnp.broadcast_to(o_ref[...], (8, tok))))
    decay = cum[0:1, tok - 1:tok]
    a_last = top_row[0:1, tok - 1:tok]
    kw_row = jnp.exp(a_row - a_last)
    rows = lax.broadcasted_iota(jnp.int32, (128, tok), 0)
    stack = jnp.where(rows == 0, top_row[0:1], jnp.where(rows == 1, cum[0:1],
            jnp.where(rows == 2, sig[0:1], kw_row[0:1])))
    cols[...] = jnp.transpose(stack)
    a1 = a_row[0:1]

    loads[3].wait()
    loads[4].wait()
    scaled = k_ref[...].astype(F32) * cols[:, 3:4]
    norm = jnp.sum(scaled, axis=0, keepdims=True)
    m_local = lax.dot_general(
        scaled.astype(BF16), v_ref[...], (((0,), (0,)), ((), ())), preferred_element_type=F32
    )
    for j in range(ny):
        mloc[j] = m_local[j * qr:(j + 1) * qr].astype(BF16)
    pad = [jnp.zeros((4, 128), F32)]
    stat = jnp.concatenate(
        [norm[:, 0:128], norm[:, 128:256], jnp.broadcast_to(decay, (1, 128)),
         jnp.broadcast_to(decay + a_last, (1, 128))] + pad, axis=0)
    sy[y] = stat
    ybuf[y] = mloc[y]
    for load in loads[5:]:
        load.wait()

    pl.semaphore_wait(barrier, len(partners))

    for d in range(1, ny):
        to = dev(z, yat(d), h)
        send(sy.at[y], sy.at[y], s1bs(d - 1), s1br(d - 1), to)
        send(mloc.at[yat(d)], ybuf.at[y], s1s(d - 1), s1r(d - 1), to)
    wb_first()
    wa_step(0)
    x_send(0)
    x_send(1)

    rb = tok // 4
    dens = []
    for r in range(4):
        width = (r + 1) * rb
        sl = pl.ds(r * rb, rb)
        scores = lax.dot_general(
            qbuf[h, sl, :], k_ref[0:width, :], (((1,), (1,)), ((), ())), preferred_element_type=F32
        ) * scale
        ti = lax.broadcasted_iota(jnp.int32, (rb, width), 0) + r * rb
        si = lax.broadcasted_iota(jnp.int32, (rb, width), 1)
        rel = jnp.where(ti >= si, a1[:, 0:width] - cols[sl, 0:1], -1e30)
        weighted = jnp.exp(rel) * scores
        dens.append(jnp.sum(weighted, axis=1, keepdims=True))
        nbuf[h, sl, :] = jnp.dot(
            weighted.astype(BF16), v_ref[0:width, :], preferred_element_type=F32).astype(BF16)
        x_send(2 + r)
    den_loc = jnp.concatenate(dens, axis=0)

    for d in range(1, ny):
        take(s1br(d - 1))
        take(s1r(d - 1))
    dec = [sy[j, 2:3, :] for j in range(ny)]
    tops = [sy[j, 3:4, :] for j in range(ny)]
    suffix = jnp.zeros((1, 128), F32)
    logs = [None] * ny
    for j in reversed(range(ny)):
        logs[j] = suffix + tops[j]
        suffix = suffix + dec[j]
    top_t = functools.reduce(jnp.maximum, logs)
    wts = [jnp.exp(lg - top_t) for lg in logs]
    total = sum(_wide(wts[j], lt) * ybuf[j].astype(F32) for j in range(ny))
    for t in range(nt):
        a, b = divmod(t, lt)
        o, s = divmod(t, tpo)
        tt[o, s * 16:(s + 1) * 16, :] = total[a * 16:(a + 1) * 16, b * 128:(b + 1) * 128].astype(BF16)
    norm_t = sum(wts[j] * sy[j, 0:2, :] for j in range(ny))
    stt[...] = jnp.concatenate([norm_t, suffix, top_t] + pad, axis=0)
    ta[z] = tt[z]
    sta[z] = stt[...]

    far = sorted(range(1, nz), key=lambda d: -min(d, nz - d))
    for d in far:
        to = dev(zat(d), y, h)
        send(stt, sta.at[z], s3bs(d - 1), s3br(d - 1), to)
        send(tt.at[zat(d)], ta.at[z], s3s(d - 1), s3r(d - 1), to)

    wa_across(0)
    wb_row()
    wa_step(1)
    wa_across(-1, 1)
    x_relay(0)
    x_relay(1)
    wb_step(1)
    wa_step(2)

    for d in far:
        take(s3br(d - 1))
        take(s3r(d - 1))
    state = jnp.zeros((tpo * 16, 128), F32)
    norm_p = jnp.zeros((2, 128), F32)
    top_p = jnp.full((1, 128), -1e30, F32)
    for zz in range(nz):
        pb[zz] = state.astype(BF16)
        sp[zz, 0:2, :] = norm_p
        sp[zz, 2:3, :] = top_p
        if zz + 1 < nz:
            top_p, keep, fresh = _combine_top(top_p, sta[zz, 2:3, :], sta[zz, 3:4, :])
            state = keep * state + fresh * ta[zz].astype(F32)
            norm_p = keep * norm_p + fresh * sta[zz, 0:2, :]
    pz[z] = pb[z]
    for d in far:
        send(pb.at[zat(d)], pz.at[z], s5s(d - 1), s5r(d - 1), dev(zat(d), y, h))

    wa_across(-2, 2)
    wb_step(2)
    wa_step(3)

    norm_p = sp[z, 0:2, :]
    top_p = sp[z, 2:3, :]
    keeps, freshs = [], []
    for j in range(ny):
        sm[j, 0:2, :] = norm_p
        sm[j, 2:3, :] = top_p
        if j + 1 < ny:
            top_p, keep, fresh = _combine_top(top_p, dec[j], tops[j])
            keeps.append(keep)
            freshs.append(fresh)
            norm_p = keep * norm_p + fresh * sy[j, 0:2, :]
    norm_prev = sm[y, 0:2, :]
    top_prev = sm[y, 2:3, :][:, 0:1]
    norm_row = jnp.concatenate([norm_prev[0:1], norm_prev[1:2]], axis=1)
    q_norm = jnp.sum(qbuf[h].astype(F32) * norm_row, axis=1, keepdims=True) * scale
    top_loc = cols[:, 0:1]
    top_mix = jnp.maximum(top_loc, top_prev)
    inner = jnp.exp(top_loc - top_mix)
    lift = jnp.exp(top_prev - top_mix)
    den = jnp.maximum(
        jnp.abs(inner * den_loc + lift * q_norm), jnp.exp(-(cols[:, 1:2] + top_mix)))
    gate = cols[:, 2:3] / den
    which = lax.broadcasted_iota(jnp.int32, (tok, 128), 1)
    both = jnp.where(which == 0, gate * inner, gate * (lift * scale))
    cbuf[h] = jnp.transpose(both)[0:8, :]
    for d in range(1, nh):
        send(cbuf.at[h], cbuf.at[h], cs(d - 1), cr(d - 1), (c, lax.rem(h + d, nh)))

    x_relay(2)
    wa_across(-3, 3)
    wa_relay(0)
    wb_step(3)
    wa_step(4)
    x_relay(3)

    for d in far:
        take(s5r(d - 1))
    tiles = [pz[t // tpo, (t % tpo) * 16:(t % tpo + 1) * 16, :].astype(F32) for t in range(nt)]
    state = jnp.concatenate(
        [jnp.concatenate(tiles[a * lt:(a + 1) * lt], axis=1) for a in range(qr // 16)], axis=0)
    for j in range(ny):
        mo[j] = state.astype(BF16)
        if j + 1 < ny:
            state = _wide(keeps[j], lt) * state + _wide(freshs[j], lt) * ybuf[j].astype(F32)
    own_quarter = pl.ds(pl.multiple_of(y * qr, qr), qr)
    mbuf[h, own_quarter, :] = mo[y]
    for d in range(1, ny):
        send(mo.at[yat(d)], mbuf.at[h, own_quarter, :], s6s(d - 1), s6r(d - 1), dev(z, yat(d), h))
    x_send(6)

    wb_step(4)
    wa_step(5)
    wa_across(-4, 4)
    wa_relay(-1, 1)
    x_relay(4)
    wb_step(5)
    wa_step(6)
    x_relay(5)

    for d in sorted(range(1, ny), key=lambda d: min(d, ny - d)):
        take(s6r(d - 1))
        x_send(6 + d)
    for n in range(2, 6):
        x_last(n)
    x_last(0)
    x_last(1)
    wa_across(-5, 5, -6, 6)
    wa_relay(-2, 2)
    wb_step(6)
    wa_step(7)
    wa_across(-7, 7)
    x_relay(6)
    wa_relay(-3, 3)
    order = [6] + [6 + d for d in sorted(range(1, ny), key=lambda d: min(d, ny - d))]
    wb_step(7)
    wa_step(8)
    wa_across(-8)
    for n in order[1:]:
        x_relay(n)
    wb_step(8)
    wa_relay(-4, 4, -5, 5)
    for n in order:
        x_last(n)
    wa_relay(-6, 6, -7, 7, -8)

    for d in range(1, nh):
        take(cr(d - 1))
    heads = [(0, h, None), (1, sib, 0)]
    if nx > 1:
        heads += [(2, hat(-1), None), (3, hat(-1, 1), 1), (4, hat(1), None), (5, hat(1, 1), 2),
                  (6, hat(2), None), (7, hat(2, 1), 3)]
    factors = [cbuf[hh] for _, hh, _ in heads]
    if nh < 16:
        factors += [jnp.zeros((128 - 8 * nh, tok), F32)]
    cols[...] = jnp.transpose(jnp.concatenate(factors, axis=0))
    items = range(6 + ny)
    for n, hh, slot in heads:
        if slot is not None:
            for m in items:
                take(br(slot, m))
        for r in range(2):
            sl = pl.ds(r * (tok // 2), tok // 2)
            far_part = jnp.dot(qbuf[hh, sl, :], mbuf[hh], preferred_element_type=F32)
            near = nbuf[hh, sl, :].astype(F32)
            gbuf[hh, sl, :] = (
                cols[sl, 8 * n:8 * n + 1] * near + cols[sl, 8 * n + 1:8 * n + 2] * far_part
            ).astype(BF16)

    if ny > 1:
        for j in rels:
            take(y2r(j + nf))

    for rr in range(tok // 256):
        sl = slice(rr * 256, (rr + 1) * 256)
        for buf, col in ((wa, 0), (wb, wc)):
            acc = jnp.zeros((256, wc), F32)
            for hh in range(nh):
                acc = acc + jnp.dot(
                    gbuf[hh, sl, :], buf[hh * dv:(hh + 1) * dv, :], preferred_element_type=F32)
            out_ref[sl, col:col + wc] = acc.astype(BF16)

    assert set(started) == got
    for copy in started.values():
        copy.wait_send()


def local(nz, ny, nx, queries, keys, values, input_pre, forget_pre, output_pre, w_out):
    tok, dk = queries.shape
    dv = values.shape[1]
    nh = 2 * nx
    qr = dk // ny
    tpo = (qr // 16) * (dv // 128) // nz
    v = pltpu.VMEM
    y1, z1 = max(ny - 1, 1), max(nz - 1, 1)
    items = 6 + ny
    scratch = [
        v((tok, dk), BF16), v((tok, dv), BF16), v((1, tok), F32), v((1, tok), F32), v((1, tok), F32),
        pltpu.SemaphoreType.DMA((8,)),
        v((ny, qr, dv), BF16), v((ny, qr, dv), BF16), v((ny, 8, 128), F32),
        v((nz, tpo * 16, 128), BF16), v((8, 128), F32),
        v((nz, tpo * 16, 128), BF16), v((nz, 8, 128), F32),
        v((nz, tpo * 16, 128), BF16), v((nz, 8, 128), F32),
        v((nz, tpo * 16, 128), BF16), v((ny, qr, dv), BF16), v((ny, 8, 128), F32),
        v((tok, 128), F32),
        v((nh, tok, dk), BF16), v((nh, tok, dv), BF16), v((nh, dk, dv), BF16), v((nh, 8, tok), F32),
        v((nh, tok, dv), BF16), v((nh * dv, dv // 2), BF16), v((nh * dv, dv // 2), BF16),
    ]
    counts = [(y1,)] * 4 + [(z1,)] * 6 + [(y1,)] * 2 + [(nz,)] * 4 + [(nz, 2)] * 4 + [(y1,)] * 2
    counts += [(nz,)] * 6 + [(3, items)] * 2 + [(4, items)] * 2 + [(nh,)] * 2
    scratch += [pltpu.SemaphoreType.DMA(n) for n in counts]
    return pl.pallas_call(
        functools.partial(kernel, nz, ny, nx),
        out_shape=jax.ShapeDtypeStruct((tok, dv), BF16),
        in_specs=[pl.BlockSpec(memory_space=pl.ANY)] * 7,
        out_specs=pl.BlockSpec(memory_space=pltpu.VMEM),
        scratch_shapes=scratch,
        compiler_params=pltpu.CompilerParams(
            collective_id=0, has_side_effects=True, vmem_limit_bytes=60 * 1024 * 1024),
        name="mlstm_layer",
    )(queries, keys, values, input_pre.reshape(1, tok), forget_pre.reshape(1, tok),
      output_pre.reshape(1, tok), w_out)


def solution(mesh, ny=NY):
    nz = mesh.shape["ctx"] // ny
    nx = mesh.shape["head"] // 2
    spec = P("ctx", "head")
    return jax.shard_map(
        functools.partial(local, nz, ny, nx), mesh=mesh, in_specs=(spec,) * 7, out_specs=spec,
        check_vma=False)
```

```python
import functools

import jax
import jax.numpy as jnp
from jax import lax
from jax.experimental import pallas as pl
from jax.experimental.pallas import tpu as pltpu
from jax.sharding import PartitionSpec as P

MESH = pl.DeviceIdType.MESH
F32 = jnp.float32
BF16 = jnp.bfloat16
NY = 4


def _log_sigmoid(f):
    e = jnp.exp(-jnp.abs(f))
    s = e / (2.0 + e)
    s2 = s * s
    poly = jnp.full_like(s, 1.0 / 15.0)
    for d in (13.0, 11.0, 9.0, 7.0, 5.0, 3.0, 1.0):
        poly = poly * s2 + 1.0 / d
    return jnp.minimum(f, 0.0) - 2.0 * s * poly


def _combine_top(top, decay, fresh):
    new = jnp.maximum(decay + top, fresh)
    return new, jnp.exp(decay + top - new), jnp.exp(fresh - new)


def _wide(row, n):
    return jnp.concatenate([row] * n, axis=1)


class Sems:
    def __init__(self, name, ref):
        self.name, self.ref = name, ref

    def __call__(self, *index):
        return (self.name,) + index, self.ref.at[index if len(index) > 1 else index[0]]


def kernel(nz, ny, nx, q_hbm, k_hbm, v_hbm, i_hbm, f_hbm, o_hbm, w_hbm, out_ref, *scr):
    (k_ref, v_ref, i_ref, f_ref, o_ref, ins, mloc, ybuf, sy, tt, stt, ta, sta, pb, sp, pz, mo, sm, cols,
     qbuf, nbuf, mbuf, cbuf, gbuf, wbuf, *sems) = scr
    (s1s, s1r, s1bs, s1br, s3s, s3r, s3bs, s3br, s5s, s5r, s6s, s6r, wafs, wafr, wabs, wabr,
     wbfs, wbfr, wbbs, wbbr, w0s, w0r, yps, ypr, yms, ymr, y2s, y2r, xs, xr, bs, br, cs, cr) = [
        Sems(n, ref) for n, ref in enumerate(sems)]
    tok, dk = k_ref.shape
    dv = v_ref.shape[1]
    wr = w_hbm.shape[0]
    wa_rows = 3 * wr // 4
    parts = 2 if ny > 1 else 1
    nh = 2 * nx
    qr = dk // ny
    lt = dv // 128
    nt = (qr // 16) * lt
    tpo = nt // nz
    scale = dk ** (-0.5)
    c = lax.axis_index("ctx")
    h = lax.axis_index("head")
    z, y = lax.div(c, ny), lax.rem(c, ny)
    x, core = lax.div(h, 2), lax.rem(h, 2)
    sib = h + 1 - 2 * core

    def wa_piece(dz, dy):
        return wbuf.at[zat(dz) * ny + yat(dy), 0:wa_rows, :]

    def wb_piece():
        return wbuf.at[c, wa_rows:wr, :]

    def zat(d):
        return lax.rem(z + (d + nz), nz)

    def yat(d):
        return lax.rem(y + (d + ny), ny)

    def hat(d, other=0):
        side = 1 - core if other else core
        return lax.rem(x + (d + nx), nx) * 2 + side

    def dev(zz, yy, hh):
        return (zz * ny + yy, hh)

    loads = [
        pltpu.make_async_copy(src, dst, ins.at[n]) for n, (src, dst) in enumerate((
            (f_hbm, f_ref), (i_hbm, i_ref), (o_hbm, o_ref), (w_hbm, wbuf.at[c]),
            (q_hbm, qbuf.at[h]), (k_hbm, k_ref), (v_hbm, v_ref)))
    ]
    for load in loads:
        load.start()

    started, got = {}, set()

    def send(src, dst, ss, rs, to):
        copy = pltpu.make_async_remote_copy(
            src_ref=src, dst_ref=dst, send_sem=ss[1], recv_sem=rs[1], device_id=to, device_id_type=MESH)
        started[rs[0]] = copy
        copy.start()

    def take(rs):
        got.add(rs[0])
        started[rs[0]].wait_recv()

    partners = [dev(z, yat(d), h) for d in range(1, ny)]
    partners += [dev(zat(d), y, h) for d in range(1, nz)]
    partners += [(c, lax.rem(h + d, nh)) for d in range(1, nh)]
    barrier = pltpu.get_barrier_semaphore()
    for p in partners:
        pl.semaphore_signal(barrier, inc=1, device_id=p, device_id_type=MESH)

    nf = nz // 2
    nb = nz - 1 - nf
    rels = list(range(-nf, nb + 1))

    def plane(dz, part):
        return wbuf.at[pl.ds(zat(dz) * ny + part * (ny // parts), ny // parts), wa_rows:wr, :]

    def wa_send(step, sign):
        piece = wa_piece(-sign * (step - 1), 0)
        ss, rs = (wafs, wafr) if sign > 0 else (wabs, wabr)
        send(piece, piece, ss(step - 1), rs(step - 1), dev(zat(sign), y, h))

    def wb_send(step, sign, part):
        piece = plane(-sign * (step - 1), part)
        ss, rs = (wbfs, wbfr) if sign > 0 else (wbbs, wbbr)
        send(piece, piece, ss(step - 1, part), rs(step - 1, part), dev(zat(sign), y, h))

    ways = ((1, nf, wafr, wbfr), (-1, nb, wabr, wbbr))

    def wa_step(step):
        for sign, last, ra, _ in ways:
            if 1 <= step <= last:
                take(ra(step - 1))
            if step + 1 <= last:
                wa_send(step + 1, sign)

    def wb_step(step):
        for part in range(parts):
            for sign, last, _, rb in ways:
                if 1 <= step <= last:
                    take(rb(step - 1, part))
                if step + 1 <= last:
                    wb_send(step + 1, sign, part)

    def wb_first():
        for d in range(1, ny):
            piece = wb_piece()
            send(piece, piece, w0s(d - 1), w0r(d - 1), dev(z, yat(d), h))

    def wb_row():
        for d in range(1, ny):
            take(w0r(d - 1))
        wb_step(0)

    def wa_across(*js):
        for j in js:
            if ny > 1 and j in rels:
                piece = wa_piece(j, 0)
                send(piece, piece, yps(j + nf), ypr(j + nf), dev(z, yat(1), h))
                send(piece, piece, yms(j + nf), ymr(j + nf), dev(z, yat(-1), h))

    def wa_relay(*js):
        for j in js:
            if ny > 1 and j in rels:
                take(ypr(j + nf))
                take(ymr(j + nf))
                sign = 1 if j % 2 == 0 else -1
                piece = wa_piece(j, -sign)
                send(piece, piece, y2s(j + nf), y2r(j + nf), dev(z, yat(sign), h))

    def item(n, hh):
        if n < 2:
            return qbuf.at[hh, pl.ds(n * (tok // 2), tok // 2), :]
        if n < 6:
            return nbuf.at[hh, pl.ds((n - 2) * (tok // 4), tok // 4), :]
        return mbuf.at[hh, pl.ds(pl.multiple_of(yat(6 - n) * qr, qr), qr), :]

    def onward(n):
        return 1 if n in (0, 2, 3, 6, 7) else -1

    def x_side(n, slot, hh):
        piece = item(n, hh)
        send(piece, piece, bs(slot, n), br(slot, n), (c, sib))

    def x_send(n):
        piece = item(n, h)
        if nx > 1:
            send(piece, piece, xs(0, n), xr(0, n), (c, hat(1)))
            send(piece, piece, xs(1, n), xr(1, n), (c, hat(-1)))
        x_side(n, 0, h)

    def x_relay(n):
        if nx > 1:
            for slot, d in ((0, -1), (1, 1)):
                take(xr(slot, n))
                if onward(n) == -d:
                    piece = item(n, hat(d))
                    send(piece, piece, xs(2, n), xr(2, n), (c, hat(-d)))
                x_side(n, 1 + slot, hat(d))

    def x_last(n):
        if nx > 1:
            take(xr(2, n))
            x_side(n, 3, hat(2))

    for load in loads[0:3]:
        load.wait()
    lane = lax.broadcasted_iota(jnp.int32, (8, tok), 1)
    gate_in = jnp.broadcast_to(i_ref[...], (8, tok))
    cum = _log_sigmoid(jnp.broadcast_to(f_ref[...], (8, tok)))
    sh = 1
    while sh < tok:
        cum = cum + jnp.where(lane >= sh, pltpu.roll(cum, sh, 1), 0.0)
        sh *= 2
    a_row = gate_in - cum
    top_row = a_row
    sh = 1
    while sh < tok:
        top_row = jnp.maximum(top_row, jnp.where(lane >= sh, pltpu.roll(top_row, sh, 1), -3e38))
        sh *= 2
    sig = 1.0 / (1.0 + jnp.exp(-jnp.broadcast_to(o_ref[...], (8, tok))))
    decay = cum[0:1, tok - 1:tok]
    a_last = top_row[0:1, tok - 1:tok]
    kw_row = jnp.exp(a_row - a_last)
    rows = lax.broadcasted_iota(jnp.int32, (128, tok), 0)
    stack = jnp.where(rows == 0, top_row[0:1], jnp.where(rows == 1, cum[0:1],
            jnp.where(rows == 2, sig[0:1], kw_row[0:1])))
    cols[...] = jnp.transpose(stack)
    a1 = a_row[0:1]
    loads[3].wait()
    loads[4].wait()

    pl.semaphore_wait(barrier, len(partners))
    wa_step(0)
    wb_first()
    x_send(0)
    x_send(1)
    wa_across(0)

    loads[5].wait()
    loads[6].wait()
    scaled = k_ref[...].astype(F32) * cols[:, 3:4]
    norm = jnp.sum(scaled, axis=0, keepdims=True)
    m_local = lax.dot_general(
        scaled.astype(BF16), v_ref[...], (((0,), (0,)), ((), ())), preferred_element_type=F32
    )
    for j in range(ny):
        mloc[j] = m_local[j * qr:(j + 1) * qr].astype(BF16)
    pad = [jnp.zeros((4, 128), F32)]
    stat = jnp.concatenate(
        [norm[:, 0:128], norm[:, 128:256], jnp.broadcast_to(decay, (1, 128)),
         jnp.broadcast_to(decay + a_last, (1, 128))] + pad, axis=0)
    sy[y] = stat
    ybuf[y] = mloc[y]
    for d in range(1, ny):
        to = dev(z, yat(d), h)
        send(sy.at[y], sy.at[y], s1bs(d - 1), s1br(d - 1), to)
        send(mloc.at[yat(d)], ybuf.at[y], s1s(d - 1), s1r(d - 1), to)
    wb_row()
    wa_step(1)

    rb = tok // 4
    dens = []
    for r in range(4):
        width = (r + 1) * rb
        sl = pl.ds(r * rb, rb)
        scores = lax.dot_general(
            qbuf[h, sl, :], k_ref[0:width, :], (((1,), (1,)), ((), ())), preferred_element_type=F32
        ) * scale
        ti = lax.broadcasted_iota(jnp.int32, (rb, width), 0) + r * rb
        si = lax.broadcasted_iota(jnp.int32, (rb, width), 1)
        rel = jnp.where(ti >= si, a1[:, 0:width] - cols[sl, 0:1], -1e30)
        weighted = jnp.exp(rel) * scores
        dens.append(jnp.sum(weighted, axis=1, keepdims=True))
        nbuf[h, sl, :] = jnp.dot(
            weighted.astype(BF16), v_ref[0:width, :], preferred_element_type=F32).astype(BF16)
        x_send(2 + r)
    den_loc = jnp.concatenate(dens, axis=0)

    for d in range(1, ny):
        take(s1br(d - 1))
        take(s1r(d - 1))
    dec = [sy[j, 2:3, :] for j in range(ny)]
    tops = [sy[j, 3:4, :] for j in range(ny)]
    suffix = jnp.zeros((1, 128), F32)
    logs = [None] * ny
    for j in reversed(range(ny)):
        logs[j] = suffix + tops[j]
        suffix = suffix + dec[j]
    top_t = functools.reduce(jnp.maximum, logs)
    wts = [jnp.exp(lg - top_t) for lg in logs]
    total = sum(_wide(wts[j], lt) * ybuf[j].astype(F32) for j in range(ny))
    for t in range(nt):
        a, b = divmod(t, lt)
        o, s = divmod(t, tpo)
        tt[o, s * 16:(s + 1) * 16, :] = total[a * 16:(a + 1) * 16, b * 128:(b + 1) * 128].astype(BF16)
    norm_t = sum(wts[j] * sy[j, 0:2, :] for j in range(ny))
    stt[...] = jnp.concatenate([norm_t, suffix, top_t] + pad, axis=0)
    ta[z] = tt[z]
    sta[z] = stt[...]

    far = sorted(range(1, nz), key=lambda d: -min(d, nz - d))
    for d in far:
        to = dev(zat(d), y, h)
        send(stt, sta.at[z], s3bs(d - 1), s3br(d - 1), to)
        send(tt.at[zat(d)], ta.at[z], s3s(d - 1), s3r(d - 1), to)

    wb_step(1)
    wa_step(2)
    wa_across(-1, 1, -2, 2)
    x_relay(0)
    x_relay(1)
    wb_step(2)
    wa_step(3)
    wa_relay(0)
    wb_step(3)
    wa_step(4)

    for d in far:
        take(s3br(d - 1))
        take(s3r(d - 1))
    state = jnp.zeros((tpo * 16, 128), F32)
    norm_p = jnp.zeros((2, 128), F32)
    top_p = jnp.full((1, 128), -1e30, F32)
    for zz in range(nz):
        pb[zz] = state.astype(BF16)
        sp[zz, 0:2, :] = norm_p
        sp[zz, 2:3, :] = top_p
        if zz + 1 < nz:
            top_p, keep, fresh = _combine_top(top_p, sta[zz, 2:3, :], sta[zz, 3:4, :])
            state = keep * state + fresh * ta[zz].astype(F32)
            norm_p = keep * norm_p + fresh * sta[zz, 0:2, :]
    pz[z] = pb[z]
    for d in far:
        send(pb.at[zat(d)], pz.at[z], s5s(d - 1), s5r(d - 1), dev(zat(d), y, h))

    wa_across(-3, 3)
    x_relay(2)
    wb_step(4)
    wa_step(5)

    norm_p = sp[z, 0:2, :]
    top_p = sp[z, 2:3, :]
    keeps, freshs = [], []
    for j in range(ny):
        sm[j, 0:2, :] = norm_p
        sm[j, 2:3, :] = top_p
        if j + 1 < ny:
            top_p, keep, fresh = _combine_top(top_p, dec[j], tops[j])
            keeps.append(keep)
            freshs.append(fresh)
            norm_p = keep * norm_p + fresh * sy[j, 0:2, :]
    norm_prev = sm[y, 0:2, :]
    top_prev = sm[y, 2:3, :][:, 0:1]
    norm_row = jnp.concatenate([norm_prev[0:1], norm_prev[1:2]], axis=1)
    q_norm = jnp.sum(qbuf[h].astype(F32) * norm_row, axis=1, keepdims=True) * scale
    top_loc = cols[:, 0:1]
    top_mix = jnp.maximum(top_loc, top_prev)
    inner = jnp.exp(top_loc - top_mix)
    lift = jnp.exp(top_prev - top_mix)
    den = jnp.maximum(
        jnp.abs(inner * den_loc + lift * q_norm), jnp.exp(-(cols[:, 1:2] + top_mix)))
    gate = cols[:, 2:3] / den
    which = lax.broadcasted_iota(jnp.int32, (tok, 128), 1)
    both = jnp.where(which == 0, gate * inner, gate * (lift * scale))
    cbuf[h] = jnp.transpose(both)[0:8, :]
    for d in range(1, nh):
        send(cbuf.at[h], cbuf.at[h], cs(d - 1), cr(d - 1), (c, lax.rem(h + d, nh)))

    x_relay(3)
    wb_step(5)
    wa_step(6)
    wa_across(-4, 4)
    wa_relay(-1, 1)

    for d in far:
        take(s5r(d - 1))
    tiles = [pz[t // tpo, (t % tpo) * 16:(t % tpo + 1) * 16, :].astype(F32) for t in range(nt)]
    state = jnp.concatenate(
        [jnp.concatenate(tiles[a * lt:(a + 1) * lt], axis=1) for a in range(qr // 16)], axis=0)
    for j in range(ny):
        mo[j] = state.astype(BF16)
        if j + 1 < ny:
            state = _wide(keeps[j], lt) * state + _wide(freshs[j], lt) * ybuf[j].astype(F32)
    own_quarter = pl.ds(pl.multiple_of(y * qr, qr), qr)
    mbuf[h, own_quarter, :] = mo[y]
    for d in range(1, ny):
        send(mo.at[yat(d)], mbuf.at[h, own_quarter, :], s6s(d - 1), s6r(d - 1), dev(z, yat(d), h))
    x_send(6)

    wb_step(6)
    wa_step(7)
    x_relay(4)
    x_relay(5)

    for d in sorted(range(1, ny), key=lambda d: min(d, ny - d)):
        take(s6r(d - 1))
        x_send(6 + d)
    for n in range(2, 6):
        x_last(n)
    x_last(0)
    x_last(1)
    wa_across(-5, 5, -6, 6)
    wa_relay(-2, 2)
    wb_step(7)
    wa_step(8)
    wb_step(8)
    wa_across(-7, 7, -8)
    wa_relay(-3, 3)
    order = [6] + [6 + d for d in sorted(range(1, ny), key=lambda d: min(d, ny - d))]
    for n, js in zip(order, ((-4, 4), (-5, 5), (-6, 6), (-7,))):
        x_relay(n)
        wa_relay(*js)
    wa_relay(*((7, -8) if ny > 1 else ()))
    for n in order:
        x_last(n)

    for d in range(1, nh):
        take(cr(d - 1))
    heads = [(0, h, None), (1, sib, 0)]
    if nx > 1:
        heads += [(2, hat(-1), None), (3, hat(-1, 1), 1), (4, hat(1), None), (5, hat(1, 1), 2),
                  (6, hat(2), None), (7, hat(2, 1), 3)]
    factors = [cbuf[hh] for _, hh, _ in heads]
    if nh < 16:
        factors += [jnp.zeros((128 - 8 * nh, tok), F32)]
    cols[...] = jnp.transpose(jnp.concatenate(factors, axis=0))
    items = range(6 + ny)
    for n, hh, slot in heads:
        if slot is not None:
            for m in items:
                take(br(slot, m))
        for r in range(2):
            sl = pl.ds(r * (tok // 2), tok // 2)
            far_part = jnp.dot(qbuf[hh, sl, :], mbuf[hh], preferred_element_type=F32)
            near = nbuf[hh, sl, :].astype(F32)
            gbuf[hh, sl, :] = (
                cols[sl, 8 * n:8 * n + 1] * near + cols[sl, 8 * n + 1:8 * n + 2] * far_part
            ).astype(BF16)

    if ny > 1:
        for j in rels:
            take(y2r(j + nf))

    if wr >= dv:
        weights = [wbuf[hh * dv // wr, hh * dv % wr:hh * dv % wr + dv, :] for hh in range(nh)]
    else:
        per = dv // wr
        weights = [wbuf[hh * per:(hh + 1) * per].reshape(dv, dv) for hh in range(nh)]
    for rr in range(tok // 256):
        sl = slice(rr * 256, (rr + 1) * 256)
        acc = jnp.zeros((256, dv), F32)
        for hh in range(nh):
            acc = acc + jnp.dot(gbuf[hh, sl, :], weights[hh], preferred_element_type=F32)
        out_ref[sl, :] = acc.astype(BF16)

    assert set(started) == got
    for copy in started.values():
        copy.wait_send()


def local(nz, ny, nx, queries, keys, values, input_pre, forget_pre, output_pre, w_out):
    tok, dk = queries.shape
    dv = values.shape[1]
    nh = 2 * nx
    qr = dk // ny
    tpo = (qr // 16) * (dv // 128) // nz
    v = pltpu.VMEM
    y1, z1 = max(ny - 1, 1), max(nz - 1, 1)
    items = 6 + ny
    scratch = [
        v((tok, dk), BF16), v((tok, dv), BF16), v((1, tok), F32), v((1, tok), F32), v((1, tok), F32),
        pltpu.SemaphoreType.DMA((7,)),
        v((ny, qr, dv), BF16), v((ny, qr, dv), BF16), v((ny, 8, 128), F32),
        v((nz, tpo * 16, 128), BF16), v((8, 128), F32),
        v((nz, tpo * 16, 128), BF16), v((nz, 8, 128), F32),
        v((nz, tpo * 16, 128), BF16), v((nz, 8, 128), F32),
        v((nz, tpo * 16, 128), BF16), v((ny, qr, dv), BF16), v((ny, 8, 128), F32),
        v((tok, 128), F32),
        v((nh, tok, dk), BF16), v((nh, tok, dv), BF16), v((nh, dk, dv), BF16), v((nh, 8, tok), F32),
        v((nh, tok, dv), BF16), v((nh * dv // w_out.shape[0],) + w_out.shape, BF16),
    ]
    counts = [(y1,)] * 4 + [(z1,)] * 6 + [(y1,)] * 2 + [(nz,)] * 4 + [(nz, 2)] * 4 + [(y1,)] * 2
    counts += [(nz,)] * 6 + [(3, items)] * 2 + [(4, items)] * 2 + [(nh,)] * 2
    scratch += [pltpu.SemaphoreType.DMA(n) for n in counts]
    return pl.pallas_call(
        functools.partial(kernel, nz, ny, nx),
        out_shape=jax.ShapeDtypeStruct((tok, dv), BF16),
        in_specs=[pl.BlockSpec(memory_space=pl.ANY)] * 7,
        out_specs=pl.BlockSpec(memory_space=pltpu.VMEM),
        scratch_shapes=scratch,
        compiler_params=pltpu.CompilerParams(
            collective_id=0, has_side_effects=True, vmem_limit_bytes=60 * 1024 * 1024),
        name="mlstm_layer",
    )(queries, keys, values, input_pre.reshape(1, tok), forget_pre.reshape(1, tok),
      output_pre.reshape(1, tok), w_out)


def solution(mesh, ny=NY):
    nz = mesh.shape["ctx"] // ny
    nx = mesh.shape["head"] // 2
    spec = P("ctx", "head")
    return jax.shard_map(
        functools.partial(local, nz, ny, nx), mesh=mesh, in_specs=(spec,) * 7, out_specs=spec,
        check_vma=False)
```

```python
import functools

import jax
import jax.numpy as jnp
from jax import lax
from jax.experimental import pallas as pl
from jax.experimental.pallas import tpu as pltpu
from jax.sharding import PartitionSpec as P

MESH = pl.DeviceIdType.MESH
F32 = jnp.float32
BF16 = jnp.bfloat16
NY = 4

PLAN = dict(
    s0=(("ac", 0),),
    s1=(("wb", 0), ("wa", 1)),
    s3=(("wb", 1), ("wa", 2), ("ac", -1, 1), ("xr", 0, 1), ("wb", 2), ("wa", 3)),
    s5a=(("wb", 3), ("wa", 4), ("ac", -2, 2, -3, 3)),
    s5b=(("xr", 2),),
    s6=(("wb", 4), ("wa", 5), ("ac", -4, 4), ("rl", 0, -1, 1)),
    rest=(("wb", 5), ("wa", 6), ("gh", 0), ("xr", 3, 4, 5), ("ac", -5, 5), ("rl", -2, 2), ("wb", 6), ("wa", 7),
          ("xr", 6), ("rl", -3, 3), ("ac", -6, 6), ("xl", 0, 1, 2), ("wb", 7), ("wa", 8), ("xr", 7),
          ("xl", 3, 4, 5), ("ac", -7, 7, -8), ("rl", -4, 4), ("xr", 9), ("rl", -5, 5), ("wb", 8), ("xr", 8),
          ("gh", 1), ("rl", -6, 6), ("gh", 2), ("xl", 6, 7, 9, 8), ("gh", 3), ("rl", -7, 7, -8)),
)


def _log_sigmoid(f):
    e = jnp.exp(-jnp.abs(f))
    s = e / (2.0 + e)
    s2 = s * s
    poly = jnp.full_like(s, 1.0 / 15.0)
    for d in (13.0, 11.0, 9.0, 7.0, 5.0, 3.0, 1.0):
        poly = poly * s2 + 1.0 / d
    return jnp.minimum(f, 0.0) - 2.0 * s * poly


def _combine_top(top, decay, fresh):
    new = jnp.maximum(decay + top, fresh)
    return new, jnp.exp(decay + top - new), jnp.exp(fresh - new)


def _wide(row, n):
    return jnp.concatenate([row] * n, axis=1)


class Sems:
    def __init__(self, name, ref):
        self.name, self.ref = name, ref

    def __call__(self, *index):
        return (self.name,) + index, self.ref.at[index if len(index) > 1 else index[0]]


def kernel(nz, ny, nx, q_hbm, k_hbm, v_hbm, i_hbm, f_hbm, o_hbm, w_hbm, out_ref, *scr):
    (k_ref, v_ref, i_ref, f_ref, o_ref, ins, mloc, ybuf, sy, tt, stt, ta, sta, pb, sp, pz, mo, sm, cols,
     qbuf, nbuf, mbuf, cbuf, gbuf, wbuf, *sems) = scr
    (s1s, s1r, s1bs, s1br, s3s, s3r, s3bs, s3br, s5s, s5r, s6s, s6r, wafs, wafr, wabs, wabr,
     wbfs, wbfr, wbbs, wbbr, w0s, w0r, yps, ypr, yms, ymr, y2s, y2r, xs, xr, bs, br, cs, cr) = [
        Sems(n, ref) for n, ref in enumerate(sems)]
    tok, dk = k_ref.shape
    dv = v_ref.shape[1]
    wr = w_hbm.shape[0]
    wa_rows = 3 * wr // 4
    parts = 2 if ny > 1 else 1
    nh = 2 * nx
    qr = dk // ny
    lt = dv // 128
    nt = (qr // 16) * lt
    tpo = nt // nz
    scale = dk ** (-0.5)
    c = lax.axis_index("ctx")
    h = lax.axis_index("head")
    z, y = lax.div(c, ny), lax.rem(c, ny)
    x, core = lax.div(h, 2), lax.rem(h, 2)
    sib = h + 1 - 2 * core

    def wa_piece(dz, dy):
        return wbuf.at[zat(dz) * ny + yat(dy), 0:wa_rows, :]

    def wb_piece():
        return wbuf.at[c, wa_rows:wr, :]

    def zat(d):
        return lax.rem(z + (d + nz), nz)

    def yat(d):
        return lax.rem(y + (d + ny), ny)

    def hat(d, other=0):
        side = 1 - core if other else core
        return lax.rem(x + (d + nx), nx) * 2 + side

    def dev(zz, yy, hh):
        return (zz * ny + yy, hh)

    loads = [
        pltpu.make_async_copy(src, dst, ins.at[n]) for n, (src, dst) in enumerate((
            (f_hbm, f_ref), (i_hbm, i_ref), (o_hbm, o_ref), (w_hbm, wbuf.at[c]),
            (q_hbm, qbuf.at[h]), (k_hbm, k_ref), (v_hbm, v_ref)))
    ]
    for load in loads:
        load.start()

    started, got = {}, set()

    def send(src, dst, ss, rs, to):
        copy = pltpu.make_async_remote_copy(
            src_ref=src, dst_ref=dst, send_sem=ss[1], recv_sem=rs[1], device_id=to, device_id_type=MESH)
        started[rs[0]] = copy
        copy.start()

    def take(rs):
        got.add(rs[0])
        started[rs[0]].wait_recv()

    partners = [dev(z, yat(d), h) for d in range(1, ny)]
    partners += [dev(zat(d), y, h) for d in range(1, nz)]
    partners += [(c, hat(d)) for d in range(1, nx)] + [(c, sib)]
    barrier = pltpu.get_barrier_semaphore()
    for p in partners:
        pl.semaphore_signal(barrier, inc=1, device_id=p, device_id_type=MESH)

    nf = nz // 2
    nb = nz - 1 - nf
    rels = list(range(-nf, nb + 1))

    def plane(dz, part):
        return wbuf.at[pl.ds(zat(dz) * ny + part * (ny // parts), ny // parts), wa_rows:wr, :]

    def wa_send(step, sign):
        piece = wa_piece(-sign * (step - 1), 0)
        ss, rs = (wafs, wafr) if sign > 0 else (wabs, wabr)
        send(piece, piece, ss(step - 1), rs(step - 1), dev(zat(sign), y, h))

    def wb_send(step, sign, part):
        piece = plane(-sign * (step - 1), part)
        ss, rs = (wbfs, wbfr) if sign > 0 else (wbbs, wbbr)
        send(piece, piece, ss(step - 1, part), rs(step - 1, part), dev(zat(sign), y, h))

    ways = ((1, nf, wafr, wbfr), (-1, nb, wabr, wbbr))

    def wa_step(step):
        for sign, last, ra, _ in ways:
            if 1 <= step <= last:
                take(ra(step - 1))
            if step + 1 <= last:
                wa_send(step + 1, sign)

    def wb_step(step):
        for part in range(parts):
            for sign, last, _, rb in ways:
                if 1 <= step <= last:
                    take(rb(step - 1, part))
                if step + 1 <= last:
                    wb_send(step + 1, sign, part)

    def wb_first():
        for d in range(1, ny):
            piece = wb_piece()
            send(piece, piece, w0s(d - 1), w0r(d - 1), dev(z, yat(d), h))

    def wb_row():
        for d in range(1, ny):
            take(w0r(d - 1))
        wb_step(0)

    def wa_across(*js):
        for j in js:
            if ny > 1 and j in rels:
                piece = wa_piece(j, 0)
                send(piece, piece, yps(j + nf), ypr(j + nf), dev(z, yat(1), h))
                send(piece, piece, yms(j + nf), ymr(j + nf), dev(z, yat(-1), h))

    def wa_relay(*js):
        for j in js:
            if ny > 1 and j in rels:
                take(ypr(j + nf))
                take(ymr(j + nf))
                sign = 1 if j % 2 == 0 else -1
                piece = wa_piece(j, -sign)
                send(piece, piece, y2s(j + nf), y2r(j + nf), dev(z, yat(sign), h))

    def item(n, hh):
        if n < 2:
            return qbuf.at[hh, pl.ds(n * (tok // 2), tok // 2), :]
        if n < 6:
            return nbuf.at[hh, pl.ds((n - 2) * (tok // 4), tok // 4), :]
        return mbuf.at[hh, pl.ds(pl.multiple_of(yat(6 - n) * qr, qr), qr), :]

    def onward(n):
        return 1 if n in (0, 2, 3, 6, 7) else -1

    def x_send(n):
        piece = item(n, h)
        if nx > 1:
            send(piece, piece, xs(0, n), xr(0, n), (c, hat(1)))
            send(piece, piece, xs(1, n), xr(1, n), (c, hat(-1)))

    def x_relay(n):
        if nx > 1:
            for slot, d in ((0, -1), (1, 1)):
                take(xr(slot, n))
                if onward(n) == -d:
                    piece = item(n, hat(d))
                    send(piece, piece, xs(2, n), xr(2, n), (c, hat(-d)))

    def x_last(n):
        if nx > 1:
            take(xr(2, n))

    done = set()

    def gate_columns():
        for d in range(1, nx):
            take(cr(d - 1))
        factors = [cbuf[hat(d)] for d in rounds] + [jnp.zeros((128 - 8 * nx, tok), F32)]
        cols[...] = jnp.transpose(jnp.concatenate(factors, axis=0))

    rounds = (0, -1, 1, 2) if nx > 1 else (0,)

    def gate_head(n):
        if n < nx:
            hh = hat(rounds[n])
            for r in range(2):
                sl = pl.ds(r * (tok // 2), tok // 2)
                far_part = jnp.dot(qbuf[hh, sl, :], mbuf[hh], preferred_element_type=F32)
                near = nbuf[hh, sl, :].astype(F32)
                gbuf[hh, sl, :] = (
                    cols[sl, 8 * n:8 * n + 1] * near + cols[sl, 8 * n + 1:8 * n + 2] * far_part
                ).astype(BF16)
                piece = gbuf.at[hh, sl, :]
                send(piece, piece, bs(n, r), br(n, r), (c, sib))

    ops = dict(wa=wa_step, wb=lambda n: wb_step(n) if n else wb_row(), ac=wa_across, rl=wa_relay,
               xr=x_relay, xl=x_last, gh=gate_head)

    def run(name):
        for op, *numbers in PLAN[name]:
            for n in numbers:
                if (op, n) not in done and (op not in ("xr", "xl") or n < 6 + ny):
                    done.add((op, n))
                    ops[op](n)

    for load in loads[0:3]:
        load.wait()
    lane = lax.broadcasted_iota(jnp.int32, (8, tok), 1)
    gate_in = jnp.broadcast_to(i_ref[...], (8, tok))
    cum = _log_sigmoid(jnp.broadcast_to(f_ref[...], (8, tok)))
    sh = 1
    while sh < tok:
        cum = cum + jnp.where(lane >= sh, pltpu.roll(cum, sh, 1), 0.0)
        sh *= 2
    a_row = gate_in - cum
    top_row = a_row
    sh = 1
    while sh < tok:
        top_row = jnp.maximum(top_row, jnp.where(lane >= sh, pltpu.roll(top_row, sh, 1), -3e38))
        sh *= 2
    sig = 1.0 / (1.0 + jnp.exp(-jnp.broadcast_to(o_ref[...], (8, tok))))
    decay = cum[0:1, tok - 1:tok]
    a_last = top_row[0:1, tok - 1:tok]
    kw_row = jnp.exp(a_row - a_last)
    rows = lax.broadcasted_iota(jnp.int32, (128, tok), 0)
    stack = jnp.where(rows == 0, top_row[0:1], jnp.where(rows == 1, cum[0:1],
            jnp.where(rows == 2, sig[0:1], kw_row[0:1])))
    cols[...] = jnp.transpose(stack)
    a1 = a_row[0:1]
    loads[3].wait()
    loads[4].wait()

    pl.semaphore_wait(barrier, len(partners))
    wa_step(0)
    wb_first()
    x_send(0)
    x_send(1)
    run("s0")

    loads[5].wait()
    loads[6].wait()
    scaled = k_ref[...].astype(F32) * cols[:, 3:4]
    norm = jnp.sum(scaled, axis=0, keepdims=True)
    m_local = lax.dot_general(
        scaled.astype(BF16), v_ref[...], (((0,), (0,)), ((), ())), preferred_element_type=F32
    )
    for j in range(ny):
        mloc[j] = m_local[j * qr:(j + 1) * qr].astype(BF16)
    pad = [jnp.zeros((4, 128), F32)]
    stat = jnp.concatenate(
        [norm[:, 0:128], norm[:, 128:256], jnp.broadcast_to(decay, (1, 128)),
         jnp.broadcast_to(decay + a_last, (1, 128))] + pad, axis=0)
    sy[y] = stat
    ybuf[y] = mloc[y]
    for d in range(1, ny):
        to = dev(z, yat(d), h)
        send(sy.at[y], sy.at[y], s1bs(d - 1), s1br(d - 1), to)
        send(mloc.at[yat(d)], ybuf.at[y], s1s(d - 1), s1r(d - 1), to)
    run("s1")

    rb = tok // 4
    dens = []
    for r in range(4):
        width = (r + 1) * rb
        sl = pl.ds(r * rb, rb)
        scores = lax.dot_general(
            qbuf[h, sl, :], k_ref[0:width, :], (((1,), (1,)), ((), ())), preferred_element_type=F32
        ) * scale
        ti = lax.broadcasted_iota(jnp.int32, (rb, width), 0) + r * rb
        si = lax.broadcasted_iota(jnp.int32, (rb, width), 1)
        rel = jnp.where(ti >= si, a1[:, 0:width] - cols[sl, 0:1], -1e30)
        weighted = jnp.exp(rel) * scores
        dens.append(jnp.sum(weighted, axis=1, keepdims=True))
        nbuf[h, sl, :] = jnp.dot(
            weighted.astype(BF16), v_ref[0:width, :], preferred_element_type=F32).astype(BF16)
    den_loc = jnp.concatenate(dens, axis=0)

    for d in range(1, ny):
        take(s1br(d - 1))
        take(s1r(d - 1))
    dec = [sy[j, 2:3, :] for j in range(ny)]
    tops = [sy[j, 3:4, :] for j in range(ny)]
    suffix = jnp.zeros((1, 128), F32)
    logs = [None] * ny
    for j in reversed(range(ny)):
        logs[j] = suffix + tops[j]
        suffix = suffix + dec[j]
    top_t = functools.reduce(jnp.maximum, logs)
    wts = [jnp.exp(lg - top_t) for lg in logs]
    total = sum(_wide(wts[j], lt) * ybuf[j].astype(F32) for j in range(ny))
    for t in range(nt):
        a, b = divmod(t, lt)
        o, s = divmod(t, tpo)
        tt[o, s * 16:(s + 1) * 16, :] = total[a * 16:(a + 1) * 16, b * 128:(b + 1) * 128].astype(BF16)
    norm_t = sum(wts[j] * sy[j, 0:2, :] for j in range(ny))
    stt[...] = jnp.concatenate([norm_t, suffix, top_t] + pad, axis=0)
    ta[z] = tt[z]
    sta[z] = stt[...]

    far = sorted(range(1, nz), key=lambda d: -min(d, nz - d))
    for d in far:
        to = dev(zat(d), y, h)
        send(stt, sta.at[z], s3bs(d - 1), s3br(d - 1), to)
        send(tt.at[zat(d)], ta.at[z], s3s(d - 1), s3r(d - 1), to)

    for n in range(2, 6):
        x_send(n)
    run("s3")

    for d in far:
        take(s3br(d - 1))
        take(s3r(d - 1))
    state = jnp.zeros((tpo * 16, 128), F32)
    norm_p = jnp.zeros((2, 128), F32)
    top_p = jnp.full((1, 128), -1e30, F32)
    for zz in range(nz):
        pb[zz] = state.astype(BF16)
        sp[zz, 0:2, :] = norm_p
        sp[zz, 2:3, :] = top_p
        if zz + 1 < nz:
            top_p, keep, fresh = _combine_top(top_p, sta[zz, 2:3, :], sta[zz, 3:4, :])
            state = keep * state + fresh * ta[zz].astype(F32)
            norm_p = keep * norm_p + fresh * sta[zz, 0:2, :]
    pz[z] = pb[z]
    for d in far:
        send(pb.at[zat(d)], pz.at[z], s5s(d - 1), s5r(d - 1), dev(zat(d), y, h))

    run("s5a")

    norm_p = sp[z, 0:2, :]
    top_p = sp[z, 2:3, :]
    keeps, freshs = [], []
    for j in range(ny):
        sm[j, 0:2, :] = norm_p
        sm[j, 2:3, :] = top_p
        if j + 1 < ny:
            top_p, keep, fresh = _combine_top(top_p, dec[j], tops[j])
            keeps.append(keep)
            freshs.append(fresh)
            norm_p = keep * norm_p + fresh * sy[j, 0:2, :]
    norm_prev = sm[y, 0:2, :]
    top_prev = sm[y, 2:3, :][:, 0:1]
    norm_row = jnp.concatenate([norm_prev[0:1], norm_prev[1:2]], axis=1)
    q_norm = jnp.sum(qbuf[h].astype(F32) * norm_row, axis=1, keepdims=True) * scale
    top_loc = cols[:, 0:1]
    top_mix = jnp.maximum(top_loc, top_prev)
    inner = jnp.exp(top_loc - top_mix)
    lift = jnp.exp(top_prev - top_mix)
    den = jnp.maximum(
        jnp.abs(inner * den_loc + lift * q_norm), jnp.exp(-(cols[:, 1:2] + top_mix)))
    gate = cols[:, 2:3] / den
    which = lax.broadcasted_iota(jnp.int32, (tok, 128), 1)
    both = jnp.where(which == 0, gate * inner, gate * (lift * scale))
    cbuf[h] = jnp.transpose(both)[0:8, :]
    for d in range(1, nx):
        send(cbuf.at[h], cbuf.at[h], cs(d - 1), cr(d - 1), (c, hat(d)))

    run("s5b")

    for d in far:
        take(s5r(d - 1))
    tiles = [pz[t // tpo, (t % tpo) * 16:(t % tpo + 1) * 16, :].astype(F32) for t in range(nt)]
    state = jnp.concatenate(
        [jnp.concatenate(tiles[a * lt:(a + 1) * lt], axis=1) for a in range(qr // 16)], axis=0)
    for j in range(ny):
        mo[j] = state.astype(BF16)
        if j + 1 < ny:
            state = _wide(keeps[j], lt) * state + _wide(freshs[j], lt) * ybuf[j].astype(F32)
    own_quarter = pl.ds(pl.multiple_of(y * qr, qr), qr)
    mbuf[h, own_quarter, :] = mo[y]
    for d in range(1, ny):
        send(mo.at[yat(d)], mbuf.at[h, own_quarter, :], s6s(d - 1), s6r(d - 1), dev(z, yat(d), h))
    x_send(6)

    run("s6")

    for d in sorted(range(1, ny), key=lambda d: min(d, ny - d)):
        take(s6r(d - 1))
        x_send(6 + d)
    gate_columns()
    run("rest")

    for n in range(nx):
        for r in range(2):
            take(br(n, r))
    if ny > 1:
        for j in rels:
            take(y2r(j + nf))

    if wr >= dv:
        weights = [wbuf[hh * dv // wr, hh * dv % wr:hh * dv % wr + dv, :] for hh in range(nh)]
    else:
        per = dv // wr
        weights = [wbuf[hh * per:(hh + 1) * per].reshape(dv, dv) for hh in range(nh)]
    for rr in range(tok // 256):
        sl = slice(rr * 256, (rr + 1) * 256)
        acc = jnp.zeros((256, dv), F32)
        for hh in range(nh):
            acc = acc + jnp.dot(gbuf[hh, sl, :], weights[hh], preferred_element_type=F32)
        out_ref[sl, :] = acc.astype(BF16)

    assert set(started) == got
    for copy in started.values():
        copy.wait_send()


def local(nz, ny, nx, queries, keys, values, input_pre, forget_pre, output_pre, w_out):
    tok, dk = queries.shape
    dv = values.shape[1]
    nh = 2 * nx
    qr = dk // ny
    tpo = (qr // 16) * (dv // 128) // nz
    v = pltpu.VMEM
    y1, z1 = max(ny - 1, 1), max(nz - 1, 1)
    items = 6 + ny
    scratch = [
        v((tok, dk), BF16), v((tok, dv), BF16), v((1, tok), F32), v((1, tok), F32), v((1, tok), F32),
        pltpu.SemaphoreType.DMA((7,)),
        v((ny, qr, dv), BF16), v((ny, qr, dv), BF16), v((ny, 8, 128), F32),
        v((nz, tpo * 16, 128), BF16), v((8, 128), F32),
        v((nz, tpo * 16, 128), BF16), v((nz, 8, 128), F32),
        v((nz, tpo * 16, 128), BF16), v((nz, 8, 128), F32),
        v((nz, tpo * 16, 128), BF16), v((ny, qr, dv), BF16), v((ny, 8, 128), F32),
        v((tok, 128), F32),
        v((nh, tok, dk), BF16), v((nh, tok, dv), BF16), v((nh, dk, dv), BF16), v((nh, 8, tok), F32),
        v((nh, tok, dv), BF16), v((nh * dv // w_out.shape[0],) + w_out.shape, BF16),
    ]
    counts = [(y1,)] * 4 + [(z1,)] * 6 + [(y1,)] * 2 + [(nz,)] * 4 + [(nz, 2)] * 4 + [(y1,)] * 2
    counts += [(nz,)] * 6 + [(3, items)] * 2 + [(nx, 2)] * 2 + [(nh,)] * 2
    scratch += [pltpu.SemaphoreType.DMA(n) for n in counts]
    return pl.pallas_call(
        functools.partial(kernel, nz, ny, nx),
        out_shape=jax.ShapeDtypeStruct((tok, dv), BF16),
        in_specs=[pl.BlockSpec(memory_space=pl.ANY)] * 7,
        out_specs=pl.BlockSpec(memory_space=pltpu.VMEM),
        scratch_shapes=scratch,
        compiler_params=pltpu.CompilerParams(
            collective_id=0, has_side_effects=True, vmem_limit_bytes=60 * 1024 * 1024),
        name="mlstm_layer",
    )(queries, keys, values, input_pre.reshape(1, tok), forget_pre.reshape(1, tok),
      output_pre.reshape(1, tok), w_out)


def solution(mesh, ny=NY):
    nz = mesh.shape["ctx"] // ny
    nx = mesh.shape["head"] // 2
    spec = P("ctx", "head")
    return jax.shard_map(
        functools.partial(local, nz, ny, nx), mesh=mesh, in_specs=(spec,) * 7, out_specs=spec,
        check_vma=False)
```

```python
import functools

import jax
import jax.numpy as jnp
from jax import lax
from jax.experimental import pallas as pl
from jax.experimental.pallas import tpu as pltpu
from jax.sharding import PartitionSpec as P

MESH = pl.DeviceIdType.MESH
F32 = jnp.float32
BF16 = jnp.bfloat16
NY = 4

PLAN = dict(
    gates=(("wb", 0), ("wa", 1)),
    s1=(("wb", 1), ("wa", 2)),
    s3=(("ac", -1, 1), ("wb", 2), ("wa", 3), ("xr", 0, 1), ("ac", -2, 2), ("rl", 0), ("wb", 3), ("wa", 4)),
    s5a=(("ac", -3, 3), ("wb", 4), ("wa", 5)),
    s5b=(("ac", -4, 4), ("rl", -1, 1), ("xr", 2), ("wb", 5), ("wa", 6)),
    s6=(("ac", -5, 5), ("rl", -2, 2), ("wb", 6), ("wa", 7), ("ac", -6, 6)),
    rest=(("xr", 3), ("rl", -3, 3), ("gh", 0), ("xr", 4, 5), ("wb", 7), ("wa", 8), ("ac", -7, 7, -8), ("xr", 6),
          ("rl", -4, 4), ("xl", 0, 1), ("xr", 7, 9), ("rl", -5, 5), ("xl", 2, 3, 4, 5), ("wb", 8), ("xr", 8),
          ("gh", 1), ("rl", -6, 6), ("gh", 2), ("rl", -7, 7, -8), ("xl", 6, 7, 9, 8), ("gh", 3)),
)


def _log_sigmoid(f):
    e = jnp.exp(-jnp.abs(f))
    s = e / (2.0 + e)
    s2 = s * s
    poly = jnp.full_like(s, 1.0 / 15.0)
    for d in (13.0, 11.0, 9.0, 7.0, 5.0, 3.0, 1.0):
        poly = poly * s2 + 1.0 / d
    return jnp.minimum(f, 0.0) - 2.0 * s * poly


def _combine_top(top, decay, fresh):
    new = jnp.maximum(decay + top, fresh)
    return new, jnp.exp(decay + top - new), jnp.exp(fresh - new)


def _wide(row, n):
    return jnp.concatenate([row] * n, axis=1)


class Sems:
    def __init__(self, name, ref):
        self.name, self.ref = name, ref

    def __call__(self, *index):
        return (self.name,) + index, self.ref.at[index if len(index) > 1 else index[0]]


def kernel(nz, ny, nx, q_hbm, k_hbm, v_hbm, i_hbm, f_hbm, o_hbm, w_hbm, out_ref, *scr):
    (k_ref, v_ref, i_ref, f_ref, o_ref, ins, mloc, ybuf, sy, tt, stt, ta, sta, pb, sp, pz, mo, sm, cols,
     qbuf, nbuf, mbuf, cbuf, gbuf, wbuf, *sems) = scr
    (s1s, s1r, s1bs, s1br, s3s, s3r, s3bs, s3br, s5s, s5r, s6s, s6r, wafs, wafr, wabs, wabr,
     wbfs, wbfr, wbbs, wbbr, w0s, w0r, yps, ypr, yms, ymr, y2s, y2r, xs, xr, bs, br, cs, cr) = [
        Sems(n, ref) for n, ref in enumerate(sems)]
    tok, dk = k_ref.shape
    dv = v_ref.shape[1]
    wr = w_hbm.shape[0]
    wa_rows = 3 * wr // 4
    parts = 2 if ny > 1 else 1
    nh = 2 * nx
    qr = dk // ny
    lt = dv // 128
    nt = (qr // 16) * lt
    tpo = nt // nz
    scale = dk ** (-0.5)
    c = lax.axis_index("ctx")
    h = lax.axis_index("head")
    z, y = lax.div(c, ny), lax.rem(c, ny)
    x, core = lax.div(h, 2), lax.rem(h, 2)
    sib = h + 1 - 2 * core

    def wa_piece(dz, dy):
        return wbuf.at[zat(dz) * ny + yat(dy), 0:wa_rows, :]

    def wb_piece():
        return wbuf.at[c, wa_rows:wr, :]

    def zat(d):
        return lax.rem(z + (d + nz), nz)

    def yat(d):
        return lax.rem(y + (d + ny), ny)

    def hat(d, other=0):
        side = 1 - core if other else core
        return lax.rem(x + (d + nx), nx) * 2 + side

    def dev(zz, yy, hh):
        return (zz * ny + yy, hh)

    loads = [
        pltpu.make_async_copy(src, dst, ins.at[n]) for n, (src, dst) in enumerate((
            (w_hbm, wbuf.at[c]), (f_hbm, f_ref), (i_hbm, i_ref), (o_hbm, o_ref),
            (k_hbm, k_ref), (v_hbm, v_ref), (q_hbm, qbuf.at[h])))
    ]
    for load in loads:
        load.start()

    started, got = {}, set()

    def send(src, dst, ss, rs, to):
        copy = pltpu.make_async_remote_copy(
            src_ref=src, dst_ref=dst, send_sem=ss[1], recv_sem=rs[1], device_id=to, device_id_type=MESH)
        started[rs[0]] = copy
        copy.start()

    def take(rs):
        got.add(rs[0])
        started[rs[0]].wait_recv()

    partners = [dev(z, yat(d), h) for d in range(1, ny)]
    partners += [dev(zat(d), y, h) for d in range(1, nz)]
    partners += [(c, hat(d)) for d in range(1, nx)] + [(c, sib)]
    barrier = pltpu.get_barrier_semaphore()
    for p in partners:
        pl.semaphore_signal(barrier, inc=1, device_id=p, device_id_type=MESH)

    nf = nz // 2
    nb = nz - 1 - nf
    rels = list(range(-nf, nb + 1))

    def plane(dz, part):
        return wbuf.at[pl.ds(zat(dz) * ny + part * (ny // parts), ny // parts), wa_rows:wr, :]

    def wa_send(step, sign):
        piece = wa_piece(-sign * (step - 1), 0)
        ss, rs = (wafs, wafr) if sign > 0 else (wabs, wabr)
        send(piece, piece, ss(step - 1), rs(step - 1), dev(zat(sign), y, h))

    def wb_send(step, sign, part):
        piece = plane(-sign * (step - 1), part)
        ss, rs = (wbfs, wbfr) if sign > 0 else (wbbs, wbbr)
        send(piece, piece, ss(step - 1, part), rs(step - 1, part), dev(zat(sign), y, h))

    ways = ((1, nf, wafr, wbfr), (-1, nb, wabr, wbbr))

    def wa_step(step):
        for sign, last, ra, _ in ways:
            if 1 <= step <= last:
                take(ra(step - 1))
            if step + 1 <= last:
                wa_send(step + 1, sign)

    def wb_step(step):
        for part in range(parts):
            for sign, last, _, rb in ways:
                if 1 <= step <= last:
                    take(rb(step - 1, part))
                if step + 1 <= last:
                    wb_send(step + 1, sign, part)

    def wb_first():
        for d in range(1, ny):
            piece = wb_piece()
            send(piece, piece, w0s(d - 1), w0r(d - 1), dev(z, yat(d), h))

    def wb_row():
        for d in range(1, ny):
            take(w0r(d - 1))
        wb_step(0)

    def wa_across(*js):
        for j in js:
            if ny > 1 and j in rels:
                piece = wa_piece(j, 0)
                send(piece, piece, yps(j + nf), ypr(j + nf), dev(z, yat(1), h))
                send(piece, piece, yms(j + nf), ymr(j + nf), dev(z, yat(-1), h))

    def wa_relay(*js):
        for j in js:
            if ny > 1 and j in rels:
                take(ypr(j + nf))
                take(ymr(j + nf))
                sign = 1 if j % 2 == 0 else -1
                piece = wa_piece(j, -sign)
                send(piece, piece, y2s(j + nf), y2r(j + nf), dev(z, yat(sign), h))

    def item(n, hh):
        if n < 2:
            return qbuf.at[hh, pl.ds(n * (tok // 2), tok // 2), :]
        if n < 6:
            return nbuf.at[hh, pl.ds((n - 2) * (tok // 4), tok // 4), :]
        return mbuf.at[hh, pl.ds(pl.multiple_of(yat(6 - n) * qr, qr), qr), :]

    def onward(n):
        return 1 if n in (0, 2, 3, 6, 7) else -1

    def x_send(n):
        piece = item(n, h)
        if nx > 1:
            send(piece, piece, xs(0, n), xr(0, n), (c, hat(1)))
            send(piece, piece, xs(1, n), xr(1, n), (c, hat(-1)))

    def x_relay(n):
        if nx > 1:
            for slot, d in ((0, -1), (1, 1)):
                take(xr(slot, n))
                if onward(n) == -d:
                    piece = item(n, hat(d))
                    send(piece, piece, xs(2, n), xr(2, n), (c, hat(-d)))

    def x_last(n):
        if nx > 1:
            take(xr(2, n))

    done = set()

    def gate_columns():
        for d in range(1, nx):
            take(cr(d - 1))
        factors = [cbuf[hat(d)] for d in rounds] + [jnp.zeros((128 - 8 * nx, tok), F32)]
        cols[...] = jnp.transpose(jnp.concatenate(factors, axis=0))

    rounds = (0, -1, 1, 2) if nx > 1 else (0,)

    def gate_head(n):
        if n < nx:
            hh = hat(rounds[n])
            for r in range(2):
                sl = pl.ds(r * (tok // 2), tok // 2)
                far_part = jnp.dot(qbuf[hh, sl, :], mbuf[hh], preferred_element_type=F32)
                near = nbuf[hh, sl, :].astype(F32)
                gbuf[hh, sl, :] = (
                    cols[sl, 8 * n:8 * n + 1] * near + cols[sl, 8 * n + 1:8 * n + 2] * far_part
                ).astype(BF16)
                piece = gbuf.at[hh, sl, :]
                send(piece, piece, bs(n, r), br(n, r), (c, sib))

    ops = dict(wa=wa_step, wb=lambda n: wb_step(n) if n else wb_row(), ac=wa_across, rl=wa_relay,
               xr=x_relay, xl=x_last, gh=gate_head)

    def run(name):
        for op, *numbers in PLAN[name]:
            for n in numbers:
                if (op, n) not in done and (op not in ("xr", "xl") or n < 6 + ny):
                    done.add((op, n))
                    ops[op](n)

    loads[0].wait()
    pl.semaphore_wait(barrier, len(partners))
    wa_step(0)
    wb_first()
    wa_across(0)

    for load in loads[1:4]:
        load.wait()
    lane = lax.broadcasted_iota(jnp.int32, (8, tok), 1)
    gate_in = jnp.broadcast_to(i_ref[...], (8, tok))
    cum = _log_sigmoid(jnp.broadcast_to(f_ref[...], (8, tok)))
    sh = 1
    while sh < tok:
        cum = cum + jnp.where(lane >= sh, pltpu.roll(cum, sh, 1), 0.0)
        sh *= 2
    a_row = gate_in - cum
    top_row = a_row
    sh = 1
    while sh < tok:
        top_row = jnp.maximum(top_row, jnp.where(lane >= sh, pltpu.roll(top_row, sh, 1), -3e38))
        sh *= 2
    sig = 1.0 / (1.0 + jnp.exp(-jnp.broadcast_to(o_ref[...], (8, tok))))
    decay = cum[0:1, tok - 1:tok]
    a_last = top_row[0:1, tok - 1:tok]
    kw_row = jnp.exp(a_row - a_last)
    rows = lax.broadcasted_iota(jnp.int32, (128, tok), 0)
    stack = jnp.where(rows == 0, top_row[0:1], jnp.where(rows == 1, cum[0:1],
            jnp.where(rows == 2, sig[0:1], kw_row[0:1])))
    cols[...] = jnp.transpose(stack)
    a1 = a_row[0:1]
    run("gates")

    loads[4].wait()
    loads[5].wait()
    scaled = k_ref[...].astype(F32) * cols[:, 3:4]
    norm = jnp.sum(scaled, axis=0, keepdims=True)
    m_local = lax.dot_general(
        scaled.astype(BF16), v_ref[...], (((0,), (0,)), ((), ())), preferred_element_type=F32
    )
    for j in range(ny):
        mloc[j] = m_local[j * qr:(j + 1) * qr].astype(BF16)
    pad = [jnp.zeros((4, 128), F32)]
    stat = jnp.concatenate(
        [norm[:, 0:128], norm[:, 128:256], jnp.broadcast_to(decay, (1, 128)),
         jnp.broadcast_to(decay + a_last, (1, 128))] + pad, axis=0)
    sy[y] = stat
    ybuf[y] = mloc[y]
    for d in range(1, ny):
        to = dev(z, yat(d), h)
        send(sy.at[y], sy.at[y], s1bs(d - 1), s1br(d - 1), to)
        send(mloc.at[yat(d)], ybuf.at[y], s1s(d - 1), s1r(d - 1), to)
    loads[6].wait()
    x_send(0)
    x_send(1)
    run("s1")

    rb = tok // 4
    dens = []
    for r in range(4):
        width = (r + 1) * rb
        sl = pl.ds(r * rb, rb)
        scores = lax.dot_general(
            qbuf[h, sl, :], k_ref[0:width, :], (((1,), (1,)), ((), ())), preferred_element_type=F32
        ) * scale
        ti = lax.broadcasted_iota(jnp.int32, (rb, width), 0) + r * rb
        si = lax.broadcasted_iota(jnp.int32, (rb, width), 1)
        rel = jnp.where(ti >= si, a1[:, 0:width] - cols[sl, 0:1], -1e30)
        weighted = jnp.exp(rel) * scores
        dens.append(jnp.sum(weighted, axis=1, keepdims=True))
        nbuf[h, sl, :] = jnp.dot(
            weighted.astype(BF16), v_ref[0:width, :], preferred_element_type=F32).astype(BF16)
    den_loc = jnp.concatenate(dens, axis=0)

    for d in range(1, ny):
        take(s1br(d - 1))
        take(s1r(d - 1))
    dec = [sy[j, 2:3, :] for j in range(ny)]
    tops = [sy[j, 3:4, :] for j in range(ny)]
    suffix = jnp.zeros((1, 128), F32)
    logs = [None] * ny
    for j in reversed(range(ny)):
        logs[j] = suffix + tops[j]
        suffix = suffix + dec[j]
    top_t = functools.reduce(jnp.maximum, logs)
    wts = [jnp.exp(lg - top_t) for lg in logs]
    total = sum(_wide(wts[j], lt) * ybuf[j].astype(F32) for j in range(ny))
    for t in range(nt):
        a, b = divmod(t, lt)
        o, s = divmod(t, tpo)
        tt[o, s * 16:(s + 1) * 16, :] = total[a * 16:(a + 1) * 16, b * 128:(b + 1) * 128].astype(BF16)
    norm_t = sum(wts[j] * sy[j, 0:2, :] for j in range(ny))
    stt[...] = jnp.concatenate([norm_t, suffix, top_t] + pad, axis=0)
    ta[z] = tt[z]
    sta[z] = stt[...]

    far = sorted(range(1, nz), key=lambda d: -min(d, nz - d))
    for d in far:
        to = dev(zat(d), y, h)
        send(stt, sta.at[z], s3bs(d - 1), s3br(d - 1), to)
        send(tt.at[zat(d)], ta.at[z], s3s(d - 1), s3r(d - 1), to)

    for n in range(2, 6):
        x_send(n)
    run("s3")

    for d in far:
        take(s3br(d - 1))
        take(s3r(d - 1))
    state = jnp.zeros((tpo * 16, 128), F32)
    norm_p = jnp.zeros((2, 128), F32)
    top_p = jnp.full((1, 128), -1e30, F32)
    for zz in range(nz):
        pb[zz] = state.astype(BF16)
        sp[zz, 0:2, :] = norm_p
        sp[zz, 2:3, :] = top_p
        if zz + 1 < nz:
            top_p, keep, fresh = _combine_top(top_p, sta[zz, 2:3, :], sta[zz, 3:4, :])
            state = keep * state + fresh * ta[zz].astype(F32)
            norm_p = keep * norm_p + fresh * sta[zz, 0:2, :]
    pz[z] = pb[z]
    for d in far:
        send(pb.at[zat(d)], pz.at[z], s5s(d - 1), s5r(d - 1), dev(zat(d), y, h))

    run("s5a")

    norm_p = sp[z, 0:2, :]
    top_p = sp[z, 2:3, :]
    keeps, freshs = [], []
    for j in range(ny):
        sm[j, 0:2, :] = norm_p
        sm[j, 2:3, :] = top_p
        if j + 1 < ny:
            top_p, keep, fresh = _combine_top(top_p, dec[j], tops[j])
            keeps.append(keep)
            freshs.append(fresh)
            norm_p = keep * norm_p + fresh * sy[j, 0:2, :]
    norm_prev = sm[y, 0:2, :]
    top_prev = sm[y, 2:3, :][:, 0:1]
    norm_row = jnp.concatenate([norm_prev[0:1], norm_prev[1:2]], axis=1)
    q_norm = jnp.sum(qbuf[h].astype(F32) * norm_row, axis=1, keepdims=True) * scale
    top_loc = cols[:, 0:1]
    top_mix = jnp.maximum(top_loc, top_prev)
    inner = jnp.exp(top_loc - top_mix)
    lift = jnp.exp(top_prev - top_mix)
    den = jnp.maximum(
        jnp.abs(inner * den_loc + lift * q_norm), jnp.exp(-(cols[:, 1:2] + top_mix)))
    gate = cols[:, 2:3] / den
    which = lax.broadcasted_iota(jnp.int32, (tok, 128), 1)
    both = jnp.where(which == 0, gate * inner, gate * (lift * scale))
    cbuf[h] = jnp.transpose(both)[0:8, :]
    for d in range(1, nx):
        send(cbuf.at[h], cbuf.at[h], cs(d - 1), cr(d - 1), (c, hat(d)))

    run("s5b")

    for d in far:
        take(s5r(d - 1))
    tiles = [pz[t // tpo, (t % tpo) * 16:(t % tpo + 1) * 16, :].astype(F32) for t in range(nt)]
    state = jnp.concatenate(
        [jnp.concatenate(tiles[a * lt:(a + 1) * lt], axis=1) for a in range(qr // 16)], axis=0)
    for j in range(ny):
        mo[j] = state.astype(BF16)
        if j + 1 < ny:
            state = _wide(keeps[j], lt) * state + _wide(freshs[j], lt) * ybuf[j].astype(F32)
    own_quarter = pl.ds(pl.multiple_of(y * qr, qr), qr)
    mbuf[h, own_quarter, :] = mo[y]
    for d in range(1, ny):
        send(mo.at[yat(d)], mbuf.at[h, own_quarter, :], s6s(d - 1), s6r(d - 1), dev(z, yat(d), h))
    x_send(6)

    run("s6")

    for d in sorted(range(1, ny), key=lambda d: min(d, ny - d)):
        take(s6r(d - 1))
        x_send(6 + d)
    gate_columns()
    run("rest")

    for n in range(nx):
        for r in range(2):
            take(br(n, r))
    if ny > 1:
        for j in rels:
            take(y2r(j + nf))

    if wr >= dv:
        weights = [wbuf[hh * dv // wr, hh * dv % wr:hh * dv % wr + dv, :] for hh in range(nh)]
    else:
        per = dv // wr
        weights = [wbuf[hh * per:(hh + 1) * per].reshape(dv, dv) for hh in range(nh)]
    for rr in range(tok // 256):
        sl = slice(rr * 256, (rr + 1) * 256)
        acc = jnp.zeros((256, dv), F32)
        for hh in range(nh):
            acc = acc + jnp.dot(gbuf[hh, sl, :], weights[hh], preferred_element_type=F32)
        out_ref[sl, :] = acc.astype(BF16)

    assert set(started) == got
    for copy in started.values():
        copy.wait_send()


def local(nz, ny, nx, queries, keys, values, input_pre, forget_pre, output_pre, w_out):
    tok, dk = queries.shape
    dv = values.shape[1]
    nh = 2 * nx
    qr = dk // ny
    tpo = (qr // 16) * (dv // 128) // nz
    v = pltpu.VMEM
    y1, z1 = max(ny - 1, 1), max(nz - 1, 1)
    items = 6 + ny
    scratch = [
        v((tok, dk), BF16), v((tok, dv), BF16), v((1, tok), F32), v((1, tok), F32), v((1, tok), F32),
        pltpu.SemaphoreType.DMA((7,)),
        v((ny, qr, dv), BF16), v((ny, qr, dv), BF16), v((ny, 8, 128), F32),
        v((nz, tpo * 16, 128), BF16), v((8, 128), F32),
        v((nz, tpo * 16, 128), BF16), v((nz, 8, 128), F32),
        v((nz, tpo * 16, 128), BF16), v((nz, 8, 128), F32),
        v((nz, tpo * 16, 128), BF16), v((ny, qr, dv), BF16), v((ny, 8, 128), F32),
        v((tok, 128), F32),
        v((nh, tok, dk), BF16), v((nh, tok, dv), BF16), v((nh, dk, dv), BF16), v((nh, 8, tok), F32),
        v((nh, tok, dv), BF16), v((nh * dv // w_out.shape[0],) + w_out.shape, BF16),
    ]
    counts = [(y1,)] * 4 + [(z1,)] * 6 + [(y1,)] * 2 + [(nz,)] * 4 + [(nz, 2)] * 4 + [(y1,)] * 2
    counts += [(nz,)] * 6 + [(3, items)] * 2 + [(nx, 2)] * 2 + [(nh,)] * 2
    scratch += [pltpu.SemaphoreType.DMA(n) for n in counts]
    return pl.pallas_call(
        functools.partial(kernel, nz, ny, nx),
        out_shape=jax.ShapeDtypeStruct((tok, dv), BF16),
        in_specs=[pl.BlockSpec(memory_space=pl.ANY)] * 7,
        out_specs=pl.BlockSpec(memory_space=pltpu.VMEM),
        scratch_shapes=scratch,
        compiler_params=pltpu.CompilerParams(
            collective_id=0, has_side_effects=True, vmem_limit_bytes=60 * 1024 * 1024),
        name="mlstm_layer",
    )(queries, keys, values, input_pre.reshape(1, tok), forget_pre.reshape(1, tok),
      output_pre.reshape(1, tok), w_out)


def solution(mesh, ny=NY):
    nz = mesh.shape["ctx"] // ny
    nx = mesh.shape["head"] // 2
    spec = P("ctx", "head")
    return jax.shard_map(
        functools.partial(local, nz, ny, nx), mesh=mesh, in_specs=(spec,) * 7, out_specs=spec,
        check_vma=False)
```

```python
import functools

import jax
import jax.numpy as jnp
from jax import lax
from jax.experimental import pallas as pl
from jax.experimental.pallas import tpu as pltpu
from jax.sharding import PartitionSpec as P

MESH = pl.DeviceIdType.MESH
F32 = jnp.float32
BF16 = jnp.bfloat16
NY = 4

PLAN = dict(
    gates=(("wb", 0), ("wa", 1)),
    s1=(("wb", 1), ("wa", 2)),
    s3=(("ac", -1, 1), ("wb", 2), ("wa", 3), ("xr", 0, 1), ("ac", -2, 2), ("rl", 0), ("wb", 3), ("wa", 4)),
    s5a=(("ac", -3, 3), ("wb", 4), ("wa", 5)),
    s5b=(("ac", -4, 4), ("rl", -1, 1), ("xr", 2), ("wb", 5), ("wa", 6)),
    s6=(("ac", -5, 5), ("rl", -2, 2), ("wb", 6), ("wa", 7), ("ac", -6, 6)),
    rest=(("xr", 3), ("rl", -3, 3), ("gh", 0), ("xr", 4, 5), ("wb", 7), ("wa", 8), ("ac", -7, 7, -8), ("xr", 6),
          ("rl", -4, 4, -5, 5), ("xl", 0, 1, 2, 3, 4, 5), ("xr", 7, 9), ("rl", -6, 6), ("xl", 6), ("rl", -7, 7, -8),
          ("xr", 8), ("gh", 1, 2), ("xl", 7, 9, 8), ("gh", 3), ("wb", 8)),
)


def _log_sigmoid(f):
    e = jnp.exp(-jnp.abs(f))
    s = e / (2.0 + e)
    s2 = s * s
    poly = jnp.full_like(s, 1.0 / 15.0)
    for d in (13.0, 11.0, 9.0, 7.0, 5.0, 3.0, 1.0):
        poly = poly * s2 + 1.0 / d
    return jnp.minimum(f, 0.0) - 2.0 * s * poly


def _combine_top(top, decay, fresh):
    new = jnp.maximum(decay + top, fresh)
    return new, jnp.exp(decay + top - new), jnp.exp(fresh - new)


def _wide(row, n):
    return jnp.concatenate([row] * n, axis=1)


class Sems:
    def __init__(self, name, ref):
        self.name, self.ref = name, ref

    def __call__(self, *index):
        return (self.name,) + index, self.ref.at[index if len(index) > 1 else index[0]]


def kernel(nz, ny, nx, q_hbm, k_hbm, v_hbm, i_hbm, f_hbm, o_hbm, w_hbm, out_ref, *scr):
    (k_ref, v_ref, i_ref, f_ref, o_ref, ins, mloc, ybuf, sy, tt, stt, ta, sta, pb, sp, pz, mo, sm, cols,
     qbuf, nbuf, mbuf, cbuf, gbuf, wbuf, acc, *sems) = scr
    (s1s, s1r, s1bs, s1br, s3s, s3r, s3bs, s3br, s5s, s5r, s6s, s6r, wafs, wafr, wabs, wabr,
     wbfs, wbfr, wbbs, wbbr, w0s, w0r, yps, ypr, yms, ymr, y2s, y2r, xs, xr, bs, br, cs, cr) = [
        Sems(n, ref) for n, ref in enumerate(sems)]
    tok, dk = k_ref.shape
    dv = v_ref.shape[1]
    wr = w_hbm.shape[0]
    wa_rows = 3 * wr // 4
    parts = 2 if ny > 1 else 1
    nh = 2 * nx
    qr = dk // ny
    lt = dv // 128
    nt = (qr // 16) * lt
    tpo = nt // nz
    scale = dk ** (-0.5)
    c = lax.axis_index("ctx")
    h = lax.axis_index("head")
    z, y = lax.div(c, ny), lax.rem(c, ny)
    x, core = lax.div(h, 2), lax.rem(h, 2)
    sib = h + 1 - 2 * core

    def wa_piece(dz, dy):
        return wbuf.at[zat(dz) * ny + yat(dy), 0:wa_rows, :]

    def wb_piece():
        return wbuf.at[c, wa_rows:wr, :]

    def zat(d):
        return lax.rem(z + (d + nz), nz)

    def yat(d):
        return lax.rem(y + (d + ny), ny)

    def hat(d, other=0):
        side = 1 - core if other else core
        return lax.rem(x + (d + nx), nx) * 2 + side

    def dev(zz, yy, hh):
        return (zz * ny + yy, hh)

    loads = [
        pltpu.make_async_copy(src, dst, ins.at[n]) for n, (src, dst) in enumerate((
            (w_hbm, wbuf.at[c]), (f_hbm, f_ref), (i_hbm, i_ref), (o_hbm, o_ref),
            (k_hbm, k_ref), (v_hbm, v_ref), (q_hbm, qbuf.at[h])))
    ]
    for load in loads:
        load.start()

    started, got = {}, set()

    def send(src, dst, ss, rs, to):
        copy = pltpu.make_async_remote_copy(
            src_ref=src, dst_ref=dst, send_sem=ss[1], recv_sem=rs[1], device_id=to, device_id_type=MESH)
        started[rs[0]] = copy
        copy.start()

    def take(rs):
        got.add(rs[0])
        started[rs[0]].wait_recv()

    partners = [dev(z, yat(d), h) for d in range(1, ny)]
    partners += [dev(zat(d), y, h) for d in range(1, nz)]
    partners += [(c, hat(d)) for d in range(1, nx)] + [(c, sib)]
    barrier = pltpu.get_barrier_semaphore()
    for p in partners:
        pl.semaphore_signal(barrier, inc=1, device_id=p, device_id_type=MESH)

    nf = nz // 2
    nb = nz - 1 - nf
    rels = list(range(-nf, nb + 1))

    def plane(dz, part):
        return wbuf.at[pl.ds(zat(dz) * ny + part * (ny // parts), ny // parts), wa_rows:wr, :]

    def wa_send(step, sign):
        piece = wa_piece(-sign * (step - 1), 0)
        ss, rs = (wafs, wafr) if sign > 0 else (wabs, wabr)
        send(piece, piece, ss(step - 1), rs(step - 1), dev(zat(sign), y, h))

    def wb_send(step, sign, part):
        piece = plane(-sign * (step - 1), part)
        ss, rs = (wbfs, wbfr) if sign > 0 else (wbbs, wbbr)
        send(piece, piece, ss(step - 1, part), rs(step - 1, part), dev(zat(sign), y, h))

    ways = ((1, nf, wafr, wbfr), (-1, nb, wabr, wbbr))

    def wa_step(step):
        for sign, last, ra, _ in ways:
            if 1 <= step <= last:
                take(ra(step - 1))
            if step + 1 <= last:
                wa_send(step + 1, sign)

    def wb_step(step):
        for part in range(parts):
            for sign, last, _, rb in ways:
                if 1 <= step <= last:
                    take(rb(step - 1, part))
                if step + 1 <= last:
                    wb_send(step + 1, sign, part)

    def wb_first():
        for d in range(1, ny):
            piece = wb_piece()
            send(piece, piece, w0s(d - 1), w0r(d - 1), dev(z, yat(d), h))

    def wb_row():
        for d in range(1, ny):
            take(w0r(d - 1))
        wb_step(0)

    def wa_across(*js):
        for j in js:
            if ny > 1 and j in rels:
                piece = wa_piece(j, 0)
                send(piece, piece, yps(j + nf), ypr(j + nf), dev(z, yat(1), h))
                send(piece, piece, yms(j + nf), ymr(j + nf), dev(z, yat(-1), h))

    def wa_relay(*js):
        for j in js:
            if ny > 1 and j in rels:
                take(ypr(j + nf))
                take(ymr(j + nf))
                sign = 1 if j % 2 == 0 else -1
                piece = wa_piece(j, -sign)
                send(piece, piece, y2s(j + nf), y2r(j + nf), dev(z, yat(sign), h))

    def item(n, hh):
        if n < 2:
            return qbuf.at[hh, pl.ds(n * (tok // 2), tok // 2), :]
        if n < 6:
            return nbuf.at[hh, pl.ds((n - 2) * (tok // 4), tok // 4), :]
        return mbuf.at[hh, pl.ds(pl.multiple_of(yat(6 - n) * qr, qr), qr), :]

    def onward(n):
        return 1 if n in (0, 2, 3, 6, 7) else -1

    def x_send(n):
        piece = item(n, h)
        if nx > 1:
            send(piece, piece, xs(0, n), xr(0, n), (c, hat(1)))
            send(piece, piece, xs(1, n), xr(1, n), (c, hat(-1)))

    def x_relay(n):
        if nx > 1:
            for slot, d in ((0, -1), (1, 1)):
                take(xr(slot, n))
                if onward(n) == -d:
                    piece = item(n, hat(d))
                    send(piece, piece, xs(2, n), xr(2, n), (c, hat(-d)))

    def x_last(n):
        if nx > 1:
            take(xr(2, n))

    done = set()

    def gate_columns():
        for d in range(1, nx):
            take(cr(d - 1))
        factors = [cbuf[hat(d)] for d in rounds] + [jnp.zeros((128 - 8 * nx, tok), F32)]
        cols[...] = jnp.transpose(jnp.concatenate(factors, axis=0))

    rounds = (0, -1, 1, 2) if nx > 1 else (0,)

    def gate_head(n):
        if n < nx:
            hh = hat(rounds[n])
            for r in range(2):
                sl = pl.ds(r * (tok // 2), tok // 2)
                far_part = jnp.dot(qbuf[hh, sl, :], mbuf[hh], preferred_element_type=F32)
                near = nbuf[hh, sl, :].astype(F32)
                gbuf[hh, sl, :] = (
                    cols[sl, 8 * n:8 * n + 1] * near + cols[sl, 8 * n + 1:8 * n + 2] * far_part
                ).astype(BF16)
                piece = gbuf.at[hh, sl, :]
                send(piece, piece, bs(n, r), br(n, r), (c, sib))

    ops = dict(wa=wa_step, wb=lambda n: wb_step(n) if n else wb_row(), ac=wa_across, rl=wa_relay,
               xr=x_relay, xl=x_last, gh=gate_head)

    def run(name):
        for op, *numbers in PLAN[name]:
            for n in numbers:
                if (op, n) not in done and (op not in ("xr", "xl") or n < 6 + ny):
                    done.add((op, n))
                    ops[op](n)

    loads[0].wait()
    pl.semaphore_wait(barrier, len(partners))
    wa_step(0)
    wb_first()
    wa_across(0)

    for load in loads[1:4]:
        load.wait()
    lane = lax.broadcasted_iota(jnp.int32, (8, tok), 1)
    gate_in = jnp.broadcast_to(i_ref[...], (8, tok))
    cum = _log_sigmoid(jnp.broadcast_to(f_ref[...], (8, tok)))
    sh = 1
    while sh < tok:
        cum = cum + jnp.where(lane >= sh, pltpu.roll(cum, sh, 1), 0.0)
        sh *= 2
    a_row = gate_in - cum
    top_row = a_row
    sh = 1
    while sh < tok:
        top_row = jnp.maximum(top_row, jnp.where(lane >= sh, pltpu.roll(top_row, sh, 1), -3e38))
        sh *= 2
    sig = 1.0 / (1.0 + jnp.exp(-jnp.broadcast_to(o_ref[...], (8, tok))))
    decay = cum[0:1, tok - 1:tok]
    a_last = top_row[0:1, tok - 1:tok]
    kw_row = jnp.exp(a_row - a_last)
    rows = lax.broadcasted_iota(jnp.int32, (128, tok), 0)
    stack = jnp.where(rows == 0, top_row[0:1], jnp.where(rows == 1, cum[0:1],
            jnp.where(rows == 2, sig[0:1], kw_row[0:1])))
    cols[...] = jnp.transpose(stack)
    a1 = a_row[0:1]
    run("gates")

    loads[4].wait()
    loads[5].wait()
    scaled = k_ref[...].astype(F32) * cols[:, 3:4]
    norm = jnp.sum(scaled, axis=0, keepdims=True)
    m_local = lax.dot_general(
        scaled.astype(BF16), v_ref[...], (((0,), (0,)), ((), ())), preferred_element_type=F32
    )
    for j in range(ny):
        mloc[j] = m_local[j * qr:(j + 1) * qr].astype(BF16)
    pad = [jnp.zeros((4, 128), F32)]
    stat = jnp.concatenate(
        [norm[:, 0:128], norm[:, 128:256], jnp.broadcast_to(decay, (1, 128)),
         jnp.broadcast_to(decay + a_last, (1, 128))] + pad, axis=0)
    sy[y] = stat
    ybuf[y] = mloc[y]
    for d in range(1, ny):
        to = dev(z, yat(d), h)
        send(sy.at[y], sy.at[y], s1bs(d - 1), s1br(d - 1), to)
        send(mloc.at[yat(d)], ybuf.at[y], s1s(d - 1), s1r(d - 1), to)
    loads[6].wait()
    x_send(0)
    x_send(1)
    run("s1")

    rb = tok // 4
    dens = []
    for r in range(4):
        width = (r + 1) * rb
        sl = pl.ds(r * rb, rb)
        scores = lax.dot_general(
            qbuf[h, sl, :], k_ref[0:width, :], (((1,), (1,)), ((), ())), preferred_element_type=F32
        ) * scale
        ti = lax.broadcasted_iota(jnp.int32, (rb, width), 0) + r * rb
        si = lax.broadcasted_iota(jnp.int32, (rb, width), 1)
        rel = jnp.where(ti >= si, a1[:, 0:width] - cols[sl, 0:1], -1e30)
        weighted = jnp.exp(rel) * scores
        dens.append(jnp.sum(weighted, axis=1, keepdims=True))
        nbuf[h, sl, :] = jnp.dot(
            weighted.astype(BF16), v_ref[0:width, :], preferred_element_type=F32).astype(BF16)
    den_loc = jnp.concatenate(dens, axis=0)

    for d in range(1, ny):
        take(s1br(d - 1))
        take(s1r(d - 1))
    dec = [sy[j, 2:3, :] for j in range(ny)]
    tops = [sy[j, 3:4, :] for j in range(ny)]
    suffix = jnp.zeros((1, 128), F32)
    logs = [None] * ny
    for j in reversed(range(ny)):
        logs[j] = suffix + tops[j]
        suffix = suffix + dec[j]
    top_t = functools.reduce(jnp.maximum, logs)
    wts = [jnp.exp(lg - top_t) for lg in logs]
    total = sum(_wide(wts[j], lt) * ybuf[j].astype(F32) for j in range(ny))
    for t in range(nt):
        a, b = divmod(t, lt)
        o, s = divmod(t, tpo)
        tt[o, s * 16:(s + 1) * 16, :] = total[a * 16:(a + 1) * 16, b * 128:(b + 1) * 128].astype(BF16)
    norm_t = sum(wts[j] * sy[j, 0:2, :] for j in range(ny))
    stt[...] = jnp.concatenate([norm_t, suffix, top_t] + pad, axis=0)
    ta[z] = tt[z]
    sta[z] = stt[...]

    far = sorted(range(1, nz), key=lambda d: -min(d, nz - d))
    for d in far:
        to = dev(zat(d), y, h)
        send(stt, sta.at[z], s3bs(d - 1), s3br(d - 1), to)
        send(tt.at[zat(d)], ta.at[z], s3s(d - 1), s3r(d - 1), to)

    for n in range(2, 6):
        x_send(n)
    run("s3")

    for d in far:
        take(s3br(d - 1))
        take(s3r(d - 1))
    state = jnp.zeros((tpo * 16, 128), F32)
    norm_p = jnp.zeros((2, 128), F32)
    top_p = jnp.full((1, 128), -1e30, F32)
    for zz in range(nz):
        pb[zz] = state.astype(BF16)
        sp[zz, 0:2, :] = norm_p
        sp[zz, 2:3, :] = top_p
        if zz + 1 < nz:
            top_p, keep, fresh = _combine_top(top_p, sta[zz, 2:3, :], sta[zz, 3:4, :])
            state = keep * state + fresh * ta[zz].astype(F32)
            norm_p = keep * norm_p + fresh * sta[zz, 0:2, :]
    pz[z] = pb[z]
    for d in far:
        send(pb.at[zat(d)], pz.at[z], s5s(d - 1), s5r(d - 1), dev(zat(d), y, h))

    run("s5a")

    norm_p = sp[z, 0:2, :]
    top_p = sp[z, 2:3, :]
    keeps, freshs = [], []
    for j in range(ny):
        sm[j, 0:2, :] = norm_p
        sm[j, 2:3, :] = top_p
        if j + 1 < ny:
            top_p, keep, fresh = _combine_top(top_p, dec[j], tops[j])
            keeps.append(keep)
            freshs.append(fresh)
            norm_p = keep * norm_p + fresh * sy[j, 0:2, :]
    norm_prev = sm[y, 0:2, :]
    top_prev = sm[y, 2:3, :][:, 0:1]
    norm_row = jnp.concatenate([norm_prev[0:1], norm_prev[1:2]], axis=1)
    q_norm = jnp.sum(qbuf[h].astype(F32) * norm_row, axis=1, keepdims=True) * scale
    top_loc = cols[:, 0:1]
    top_mix = jnp.maximum(top_loc, top_prev)
    inner = jnp.exp(top_loc - top_mix)
    lift = jnp.exp(top_prev - top_mix)
    den = jnp.maximum(
        jnp.abs(inner * den_loc + lift * q_norm), jnp.exp(-(cols[:, 1:2] + top_mix)))
    gate = cols[:, 2:3] / den
    which = lax.broadcasted_iota(jnp.int32, (tok, 128), 1)
    both = jnp.where(which == 0, gate * inner, gate * (lift * scale))
    cbuf[h] = jnp.transpose(both)[0:8, :]
    for d in range(1, nx):
        send(cbuf.at[h], cbuf.at[h], cs(d - 1), cr(d - 1), (c, hat(d)))

    run("s5b")

    for d in far:
        take(s5r(d - 1))
    tiles = [pz[t // tpo, (t % tpo) * 16:(t % tpo + 1) * 16, :].astype(F32) for t in range(nt)]
    state = jnp.concatenate(
        [jnp.concatenate(tiles[a * lt:(a + 1) * lt], axis=1) for a in range(qr // 16)], axis=0)
    for j in range(ny):
        mo[j] = state.astype(BF16)
        if j + 1 < ny:
            state = _wide(keeps[j], lt) * state + _wide(freshs[j], lt) * ybuf[j].astype(F32)
    own_quarter = pl.ds(pl.multiple_of(y * qr, qr), qr)
    mbuf[h, own_quarter, :] = mo[y]
    for d in range(1, ny):
        send(mo.at[yat(d)], mbuf.at[h, own_quarter, :], s6s(d - 1), s6r(d - 1), dev(z, yat(d), h))
    x_send(6)

    run("s6")

    for d in sorted(range(1, ny), key=lambda d: min(d, ny - d)):
        take(s6r(d - 1))
        x_send(6 + d)
    gate_columns()
    run("rest")

    if ny > 1:
        for j in rels:
            take(y2r(j + nf))

    def weights(hh):
        if wr >= dv:
            row = pl.multiple_of(lax.rem(hh * dv, wr), dv)
            return wbuf[lax.div(hh * dv, wr), pl.ds(row, dv), :]
        return wbuf[pl.ds(hh * (dv // wr), dv // wr)].reshape(dv, dv)

    def project(sl, other):
        return sum(
            jnp.dot(gbuf[hat(d, other), sl, :], weights(hat(d, other)), preferred_element_type=F32)
            for d in rounds)

    row_halves = [pl.ds(r * (tok // 2), tok // 2) for r in range(2)]
    for sl in row_halves:
        acc[sl, :] = project(sl, 0)
    for n in range(nx):
        for r in range(2):
            take(br(n, r))
    for sl in row_halves:
        out_ref[sl, :] = (acc[sl, :] + project(sl, 1)).astype(BF16)

    assert set(started) == got
    for copy in started.values():
        copy.wait_send()


def local(nz, ny, nx, queries, keys, values, input_pre, forget_pre, output_pre, w_out):
    tok, dk = queries.shape
    dv = values.shape[1]
    nh = 2 * nx
    qr = dk // ny
    tpo = (qr // 16) * (dv // 128) // nz
    v = pltpu.VMEM
    y1, z1 = max(ny - 1, 1), max(nz - 1, 1)
    items = 6 + ny
    scratch = [
        v((tok, dk), BF16), v((tok, dv), BF16), v((1, tok), F32), v((1, tok), F32), v((1, tok), F32),
        pltpu.SemaphoreType.DMA((7,)),
        v((ny, qr, dv), BF16), v((ny, qr, dv), BF16), v((ny, 8, 128), F32),
        v((nz, tpo * 16, 128), BF16), v((8, 128), F32),
        v((nz, tpo * 16, 128), BF16), v((nz, 8, 128), F32),
        v((nz, tpo * 16, 128), BF16), v((nz, 8, 128), F32),
        v((nz, tpo * 16, 128), BF16), v((ny, qr, dv), BF16), v((ny, 8, 128), F32),
        v((tok, 128), F32),
        v((nh, tok, dk), BF16), v((nh, tok, dv), BF16), v((nh, dk, dv), BF16), v((nh, 8, tok), F32),
        v((nh, tok, dv), BF16), v((nh * dv // w_out.shape[0],) + w_out.shape, BF16),
        v((tok, dv), F32),
    ]
    counts = [(y1,)] * 4 + [(z1,)] * 6 + [(y1,)] * 2 + [(nz,)] * 4 + [(nz, 2)] * 4 + [(y1,)] * 2
    counts += [(nz,)] * 6 + [(3, items)] * 2 + [(nx, 2)] * 2 + [(nh,)] * 2
    scratch += [pltpu.SemaphoreType.DMA(n) for n in counts]
    return pl.pallas_call(
        functools.partial(kernel, nz, ny, nx),
        out_shape=jax.ShapeDtypeStruct((tok, dv), BF16),
        in_specs=[pl.BlockSpec(memory_space=pl.ANY)] * 7,
        out_specs=pl.BlockSpec(memory_space=pltpu.VMEM),
        scratch_shapes=scratch,
        compiler_params=pltpu.CompilerParams(
            collective_id=0, has_side_effects=True, vmem_limit_bytes=60 * 1024 * 1024),
        name="mlstm_layer",
    )(queries, keys, values, input_pre.reshape(1, tok), forget_pre.reshape(1, tok),
      output_pre.reshape(1, tok), w_out)


def solution(mesh, ny=NY):
    nz = mesh.shape["ctx"] // ny
    nx = mesh.shape["head"] // 2
    spec = P("ctx", "head")
    return jax.shard_map(
        functools.partial(local, nz, ny, nx), mesh=mesh, in_specs=(spec,) * 7, out_specs=spec,
        check_vma=False)
```

```python
import functools

import jax
import jax.numpy as jnp
from jax import lax
from jax.experimental import pallas as pl
from jax.experimental.pallas import tpu as pltpu
from jax.sharding import PartitionSpec as P

MESH = pl.DeviceIdType.MESH
F32 = jnp.float32
BF16 = jnp.bfloat16
NY = 4

PLAN = dict(
    gates=(("wb", 0), ("wa", 1)),
    s1=(("wb", 1), ("wa", 2)),
    s3=(("ac", -1, 1), ("wb", 2), ("wa", 3), ("xr", 0, 1), ("ac", -2, 2), ("rl", 0), ("wb", 3), ("wa", 4)),
    s5a=(("ac", -3, 3), ("wb", 4), ("wa", 5)),
    s5b=(("ac", -4, 4), ("rl", -1, 1), ("xr", 2), ("wb", 5), ("wa", 6)),
    s6=(("ac", -5, 5), ("rl", -2, 2), ("wb", 6), ("wa", 7), ("ac", -6, 6)),
    rest=(("xr", 3), ("rl", -3, 3), ("gh", 0), ("xr", 4, 5), ("wb", 7), ("wa", 8), ("ac", -7, 7, -8), ("xr", 6),
          ("rl", -4, 4, -5, 5), ("xl", 0, 1, 2, 3, 4, 5), ("xr", 7, 9), ("rl", -6, 6), ("xl", 6), ("rl", -7, 7, -8),
          ("xr", 8), ("gh", 1, 2), ("xl", 7, 9, 8), ("gh", 3), ("wb", 8)),
)


def _log_sigmoid(f):
    e = jnp.exp(-jnp.abs(f))
    s = e / (2.0 + e)
    s2 = s * s
    poly = jnp.full_like(s, 1.0 / 15.0)
    for d in (13.0, 11.0, 9.0, 7.0, 5.0, 3.0, 1.0):
        poly = poly * s2 + 1.0 / d
    return jnp.minimum(f, 0.0) - 2.0 * s * poly


def _combine_top(top, decay, fresh):
    new = jnp.maximum(decay + top, fresh)
    return new, jnp.exp(decay + top - new), jnp.exp(fresh - new)


def _wide(row, n):
    return jnp.concatenate([row] * n, axis=1)


class Sems:
    def __init__(self, name, ref):
        self.name, self.ref = name, ref

    def __call__(self, *index):
        return (self.name,) + index, self.ref.at[index if len(index) > 1 else index[0]]


def kernel(nz, ny, nx, q_hbm, k_hbm, v_hbm, i_hbm, f_hbm, o_hbm, w_hbm, out_ref, *scr):
    (k_ref, v_ref, i_ref, f_ref, o_ref, ins, mloc, ybuf, sy, tt, stt, ta, sta, pb, sp, pz, mo, sm, cols,
     qbuf, nbuf, mbuf, cbuf, gbuf, wbuf, acc, *sems) = scr
    (s1s, s1r, s1bs, s1br, s3s, s3r, s3bs, s3br, s5s, s5r, s6s, s6r, wafs, wafr, wabs, wabr,
     wbfs, wbfr, wbbs, wbbr, w0s, w0r, yps, ypr, yms, ymr, y2s, y2r, xs, xr, bs, br, cs, cr) = [
        Sems(n, ref) for n, ref in enumerate(sems)]
    tok, dk = k_ref.shape
    dv = v_ref.shape[1]
    wr = w_hbm.shape[0]
    wa_rows = 3 * wr // 4
    parts = 2 if ny > 1 else 1
    nh = 2 * nx
    qr = dk // ny
    lt = dv // 128
    nt = (qr // 16) * lt
    tpo = nt // nz
    scale = dk ** (-0.5)
    c = lax.axis_index("ctx")
    h = lax.axis_index("head")
    z, y = lax.div(c, ny), lax.rem(c, ny)
    x, core = lax.div(h, 2), lax.rem(h, 2)
    sib = h + 1 - 2 * core

    def wa_piece(dz, dy):
        return wbuf.at[zat(dz) * ny + yat(dy), 0:wa_rows, :]

    def wb_piece():
        return wbuf.at[c, wa_rows:wr, :]

    def zat(d):
        return lax.rem(z + (d + nz), nz)

    def yat(d):
        return lax.rem(y + (d + ny), ny)

    def hat(d, other=0):
        side = 1 - core if other else core
        return lax.rem(x + (d + nx), nx) * 2 + side

    def dev(zz, yy, hh):
        return (zz * ny + yy, hh)

    loads = [
        pltpu.make_async_copy(src, dst, ins.at[n]) for n, (src, dst) in enumerate((
            (w_hbm, wbuf.at[c]), (q_hbm, qbuf.at[h]), (f_hbm, f_ref), (i_hbm, i_ref), (o_hbm, o_ref),
            (k_hbm, k_ref), (v_hbm, v_ref)))
    ]
    for load in loads:
        load.start()

    started, got = {}, set()

    def send(src, dst, ss, rs, to):
        copy = pltpu.make_async_remote_copy(
            src_ref=src, dst_ref=dst, send_sem=ss[1], recv_sem=rs[1], device_id=to, device_id_type=MESH)
        started[rs[0]] = copy
        copy.start()

    def take(rs):
        got.add(rs[0])
        started[rs[0]].wait_recv()

    partners = [dev(z, yat(d), h) for d in range(1, ny)]
    partners += [dev(zat(d), y, h) for d in range(1, nz)]
    partners += [(c, hat(d)) for d in range(1, nx)] + [(c, sib)]
    barrier = pltpu.get_barrier_semaphore()
    for p in partners:
        pl.semaphore_signal(barrier, inc=1, device_id=p, device_id_type=MESH)

    nf = nz // 2
    nb = nz - 1 - nf
    rels = list(range(-nf, nb + 1))

    def plane(dz, part):
        return wbuf.at[pl.ds(zat(dz) * ny + part * (ny // parts), ny // parts), wa_rows:wr, :]

    def wa_send(step, sign):
        piece = wa_piece(-sign * (step - 1), 0)
        ss, rs = (wafs, wafr) if sign > 0 else (wabs, wabr)
        send(piece, piece, ss(step - 1), rs(step - 1), dev(zat(sign), y, h))

    def wb_send(step, sign, part):
        piece = plane(-sign * (step - 1), part)
        ss, rs = (wbfs, wbfr) if sign > 0 else (wbbs, wbbr)
        send(piece, piece, ss(step - 1, part), rs(step - 1, part), dev(zat(sign), y, h))

    ways = ((1, nf, wafr, wbfr), (-1, nb, wabr, wbbr))

    def wa_step(step):
        for sign, last, ra, _ in ways:
            if 1 <= step <= last:
                take(ra(step - 1))
            if step + 1 <= last:
                wa_send(step + 1, sign)

    def wb_step(step):
        for part in range(parts):
            for sign, last, _, rb in ways:
                if 1 <= step <= last:
                    take(rb(step - 1, part))
                if step + 1 <= last:
                    wb_send(step + 1, sign, part)

    def wb_first():
        for d in range(1, ny):
            piece = wb_piece()
            send(piece, piece, w0s(d - 1), w0r(d - 1), dev(z, yat(d), h))

    def wb_row():
        for d in range(1, ny):
            take(w0r(d - 1))
        wb_step(0)

    def wa_across(*js):
        for j in js:
            if ny > 1 and j in rels:
                piece = wa_piece(j, 0)
                send(piece, piece, yps(j + nf), ypr(j + nf), dev(z, yat(1), h))
                send(piece, piece, yms(j + nf), ymr(j + nf), dev(z, yat(-1), h))

    def wa_relay(*js):
        for j in js:
            if ny > 1 and j in rels:
                take(ypr(j + nf))
                take(ymr(j + nf))
                sign = 1 if j % 2 == 0 else -1
                piece = wa_piece(j, -sign)
                send(piece, piece, y2s(j + nf), y2r(j + nf), dev(z, yat(sign), h))

    def item(n, hh):
        if n < 2:
            return qbuf.at[hh, pl.ds(n * (tok // 2), tok // 2), :]
        if n < 6:
            return nbuf.at[hh, pl.ds((n - 2) * (tok // 4), tok // 4), :]
        return mbuf.at[hh, pl.ds(pl.multiple_of(yat(6 - n) * qr, qr), qr), :]

    def onward(n):
        return 1 if n in (0, 2, 3, 6, 7) else -1

    def x_send(n):
        piece = item(n, h)
        if nx > 1:
            send(piece, piece, xs(0, n), xr(0, n), (c, hat(1)))
            send(piece, piece, xs(1, n), xr(1, n), (c, hat(-1)))

    def x_relay(n):
        if nx > 1:
            for slot, d in ((0, -1), (1, 1)):
                take(xr(slot, n))
                if onward(n) == -d:
                    piece = item(n, hat(d))
                    send(piece, piece, xs(2, n), xr(2, n), (c, hat(-d)))

    def x_last(n):
        if nx > 1:
            take(xr(2, n))

    done = set()

    def gate_columns():
        for d in range(1, nx):
            take(cr(d - 1))
        factors = [cbuf[hat(d)] for d in rounds] + [jnp.zeros((128 - 8 * nx, tok), F32)]
        cols[...] = jnp.transpose(jnp.concatenate(factors, axis=0))

    rounds = (0, -1, 1, 2) if nx > 1 else (0,)

    def gate_head(n):
        if n < nx:
            hh = hat(rounds[n])
            for r in range(2):
                sl = pl.ds(r * (tok // 2), tok // 2)
                far_part = jnp.dot(qbuf[hh, sl, :], mbuf[hh], preferred_element_type=F32)
                near = nbuf[hh, sl, :].astype(F32)
                gbuf[hh, sl, :] = (
                    cols[sl, 8 * n:8 * n + 1] * near + cols[sl, 8 * n + 1:8 * n + 2] * far_part
                ).astype(BF16)
                piece = gbuf.at[hh, sl, :]
                send(piece, piece, bs(n, r), br(n, r), (c, sib))

    ops = dict(wa=wa_step, wb=lambda n: wb_step(n) if n else wb_row(), ac=wa_across, rl=wa_relay,
               xr=x_relay, xl=x_last, gh=gate_head)

    def run(name):
        for op, *numbers in PLAN[name]:
            for n in numbers:
                if (op, n) not in done and (op not in ("xr", "xl") or n < 6 + ny):
                    done.add((op, n))
                    ops[op](n)

    loads[0].wait()
    pl.semaphore_wait(barrier, len(partners))
    wa_step(0)
    wb_first()
    wa_across(0)
    loads[1].wait()
    x_send(0)
    x_send(1)

    for load in loads[2:5]:
        load.wait()
    lane = lax.broadcasted_iota(jnp.int32, (8, tok), 1)
    gate_in = jnp.broadcast_to(i_ref[...], (8, tok))
    cum = _log_sigmoid(jnp.broadcast_to(f_ref[...], (8, tok)))
    sh = 1
    while sh < tok:
        cum = cum + jnp.where(lane >= sh, pltpu.roll(cum, sh, 1), 0.0)
        sh *= 2
    a_row = gate_in - cum
    top_row = a_row
    sh = 1
    while sh < tok:
        top_row = jnp.maximum(top_row, jnp.where(lane >= sh, pltpu.roll(top_row, sh, 1), -3e38))
        sh *= 2
    sig = 1.0 / (1.0 + jnp.exp(-jnp.broadcast_to(o_ref[...], (8, tok))))
    decay = cum[0:1, tok - 1:tok]
    a_last = top_row[0:1, tok - 1:tok]
    kw_row = jnp.exp(a_row - a_last)
    rows = lax.broadcasted_iota(jnp.int32, (128, tok), 0)
    stack = jnp.where(rows == 0, top_row[0:1], jnp.where(rows == 1, cum[0:1],
            jnp.where(rows == 2, sig[0:1], kw_row[0:1])))
    cols[...] = jnp.transpose(stack)
    a1 = a_row[0:1]
    run("gates")

    loads[5].wait()
    loads[6].wait()
    scaled = k_ref[...].astype(F32) * cols[:, 3:4]
    norm = jnp.sum(scaled, axis=0, keepdims=True)
    m_local = lax.dot_general(
        scaled.astype(BF16), v_ref[...], (((0,), (0,)), ((), ())), preferred_element_type=F32
    )
    for j in range(ny):
        mloc[j] = m_local[j * qr:(j + 1) * qr].astype(BF16)
    pad = [jnp.zeros((4, 128), F32)]
    stat = jnp.concatenate(
        [norm[:, 0:128], norm[:, 128:256], jnp.broadcast_to(decay, (1, 128)),
         jnp.broadcast_to(decay + a_last, (1, 128))] + pad, axis=0)
    sy[y] = stat
    ybuf[y] = mloc[y]
    for d in range(1, ny):
        to = dev(z, yat(d), h)
        send(sy.at[y], sy.at[y], s1bs(d - 1), s1br(d - 1), to)
        send(mloc.at[yat(d)], ybuf.at[y], s1s(d - 1), s1r(d - 1), to)
    run("s1")

    rb = tok // 4
    dens = []
    for r in range(4):
        width = (r + 1) * rb
        sl = pl.ds(r * rb, rb)
        scores = lax.dot_general(
            qbuf[h, sl, :], k_ref[0:width, :], (((1,), (1,)), ((), ())), preferred_element_type=F32
        ) * scale
        ti = lax.broadcasted_iota(jnp.int32, (rb, width), 0) + r * rb
        si = lax.broadcasted_iota(jnp.int32, (rb, width), 1)
        rel = jnp.where(ti >= si, a1[:, 0:width] - cols[sl, 0:1], -1e30)
        weighted = jnp.exp(rel) * scores
        dens.append(jnp.sum(weighted, axis=1, keepdims=True))
        nbuf[h, sl, :] = jnp.dot(
            weighted.astype(BF16), v_ref[0:width, :], preferred_element_type=F32).astype(BF16)
    den_loc = jnp.concatenate(dens, axis=0)

    for d in range(1, ny):
        take(s1br(d - 1))
        take(s1r(d - 1))
    dec = [sy[j, 2:3, :] for j in range(ny)]
    tops = [sy[j, 3:4, :] for j in range(ny)]
    suffix = jnp.zeros((1, 128), F32)
    logs = [None] * ny
    for j in reversed(range(ny)):
        logs[j] = suffix + tops[j]
        suffix = suffix + dec[j]
    top_t = functools.reduce(jnp.maximum, logs)
    wts = [jnp.exp(lg - top_t) for lg in logs]
    total = sum(_wide(wts[j], lt) * ybuf[j].astype(F32) for j in range(ny))
    for t in range(nt):
        a, b = divmod(t, lt)
        o, s = divmod(t, tpo)
        tt[o, s * 16:(s + 1) * 16, :] = total[a * 16:(a + 1) * 16, b * 128:(b + 1) * 128].astype(BF16)
    norm_t = sum(wts[j] * sy[j, 0:2, :] for j in range(ny))
    stt[...] = jnp.concatenate([norm_t, suffix, top_t] + pad, axis=0)
    ta[z] = tt[z]
    sta[z] = stt[...]

    far = sorted(range(1, nz), key=lambda d: -min(d, nz - d))
    for d in far:
        to = dev(zat(d), y, h)
        send(stt, sta.at[z], s3bs(d - 1), s3br(d - 1), to)
        send(tt.at[zat(d)], ta.at[z], s3s(d - 1), s3r(d - 1), to)

    x_send(2)
    x_send(3)
    run("s3")

    for d in far:
        take(s3br(d - 1))
        take(s3r(d - 1))
    state = jnp.zeros((tpo * 16, 128), F32)
    norm_p = jnp.zeros((2, 128), F32)
    top_p = jnp.full((1, 128), -1e30, F32)
    for zz in range(nz):
        pb[zz] = state.astype(BF16)
        sp[zz, 0:2, :] = norm_p
        sp[zz, 2:3, :] = top_p
        if zz + 1 < nz:
            top_p, keep, fresh = _combine_top(top_p, sta[zz, 2:3, :], sta[zz, 3:4, :])
            state = keep * state + fresh * ta[zz].astype(F32)
            norm_p = keep * norm_p + fresh * sta[zz, 0:2, :]
    pz[z] = pb[z]
    for d in far:
        send(pb.at[zat(d)], pz.at[z], s5s(d - 1), s5r(d - 1), dev(zat(d), y, h))

    x_send(4)
    x_send(5)
    run("s5a")

    norm_p = sp[z, 0:2, :]
    top_p = sp[z, 2:3, :]
    keeps, freshs = [], []
    for j in range(ny):
        sm[j, 0:2, :] = norm_p
        sm[j, 2:3, :] = top_p
        if j + 1 < ny:
            top_p, keep, fresh = _combine_top(top_p, dec[j], tops[j])
            keeps.append(keep)
            freshs.append(fresh)
            norm_p = keep * norm_p + fresh * sy[j, 0:2, :]
    norm_prev = sm[y, 0:2, :]
    top_prev = sm[y, 2:3, :][:, 0:1]
    norm_row = jnp.concatenate([norm_prev[0:1], norm_prev[1:2]], axis=1)
    q_norm = jnp.sum(qbuf[h].astype(F32) * norm_row, axis=1, keepdims=True) * scale
    top_loc = cols[:, 0:1]
    top_mix = jnp.maximum(top_loc, top_prev)
    inner = jnp.exp(top_loc - top_mix)
    lift = jnp.exp(top_prev - top_mix)
    den = jnp.maximum(
        jnp.abs(inner * den_loc + lift * q_norm), jnp.exp(-(cols[:, 1:2] + top_mix)))
    gate = cols[:, 2:3] / den
    which = lax.broadcasted_iota(jnp.int32, (tok, 128), 1)
    both = jnp.where(which == 0, gate * inner, gate * (lift * scale))
    cbuf[h] = jnp.transpose(both)[0:8, :]
    for d in range(1, nx):
        send(cbuf.at[h], cbuf.at[h], cs(d - 1), cr(d - 1), (c, hat(d)))

    run("s5b")

    for d in far:
        take(s5r(d - 1))
    tiles = [pz[t // tpo, (t % tpo) * 16:(t % tpo + 1) * 16, :].astype(F32) for t in range(nt)]
    state = jnp.concatenate(
        [jnp.concatenate(tiles[a * lt:(a + 1) * lt], axis=1) for a in range(qr // 16)], axis=0)
    for j in range(ny):
        mo[j] = state.astype(BF16)
        if j + 1 < ny:
            state = _wide(keeps[j], lt) * state + _wide(freshs[j], lt) * ybuf[j].astype(F32)
    own_quarter = pl.ds(pl.multiple_of(y * qr, qr), qr)
    mbuf[h, own_quarter, :] = mo[y]
    for d in range(1, ny):
        send(mo.at[yat(d)], mbuf.at[h, own_quarter, :], s6s(d - 1), s6r(d - 1), dev(z, yat(d), h))
    x_send(6)

    run("s6")

    for d in sorted(range(1, ny), key=lambda d: min(d, ny - d)):
        take(s6r(d - 1))
        x_send(6 + d)
    gate_columns()
    run("rest")

    if ny > 1:
        for j in rels:
            take(y2r(j + nf))

    def weights(hh):
        if wr >= dv:
            row = pl.multiple_of(lax.rem(hh * dv, wr), dv)
            return wbuf[lax.div(hh * dv, wr), pl.ds(row, dv), :]
        return wbuf[pl.ds(hh * (dv // wr), dv // wr)].reshape(dv, dv)

    def project(sl, other):
        return sum(
            jnp.dot(gbuf[hat(d, other), sl, :], weights(hat(d, other)), preferred_element_type=F32)
            for d in rounds)

    row_halves = [pl.ds(r * (tok // 2), tok // 2) for r in range(2)]
    for sl in row_halves:
        acc[sl, :] = project(sl, 0)
    for n in range(nx):
        for r in range(2):
            take(br(n, r))
    for sl in row_halves:
        out_ref[sl, :] = (acc[sl, :] + project(sl, 1)).astype(BF16)

    assert set(started) == got
    for copy in started.values():
        copy.wait_send()


def local(nz, ny, nx, queries, keys, values, input_pre, forget_pre, output_pre, w_out):
    tok, dk = queries.shape
    dv = values.shape[1]
    nh = 2 * nx
    qr = dk // ny
    tpo = (qr // 16) * (dv // 128) // nz
    v = pltpu.VMEM
    y1, z1 = max(ny - 1, 1), max(nz - 1, 1)
    items = 6 + ny
    scratch = [
        v((tok, dk), BF16), v((tok, dv), BF16), v((1, tok), F32), v((1, tok), F32), v((1, tok), F32),
        pltpu.SemaphoreType.DMA((7,)),
        v((ny, qr, dv), BF16), v((ny, qr, dv), BF16), v((ny, 8, 128), F32),
        v((nz, tpo * 16, 128), BF16), v((8, 128), F32),
        v((nz, tpo * 16, 128), BF16), v((nz, 8, 128), F32),
        v((nz, tpo * 16, 128), BF16), v((nz, 8, 128), F32),
        v((nz, tpo * 16, 128), BF16), v((ny, qr, dv), BF16), v((ny, 8, 128), F32),
        v((tok, 128), F32),
        v((nh, tok, dk), BF16), v((nh, tok, dv), BF16), v((nh, dk, dv), BF16), v((nh, 8, tok), F32),
        v((nh, tok, dv), BF16), v((nh * dv // w_out.shape[0],) + w_out.shape, BF16),
        v((tok, dv), F32),
    ]
    counts = [(y1,)] * 4 + [(z1,)] * 6 + [(y1,)] * 2 + [(nz,)] * 4 + [(nz, 2)] * 4 + [(y1,)] * 2
    counts += [(nz,)] * 6 + [(3, items)] * 2 + [(nx, 2)] * 2 + [(nh,)] * 2
    scratch += [pltpu.SemaphoreType.DMA(n) for n in counts]
    return pl.pallas_call(
        functools.partial(kernel, nz, ny, nx),
        out_shape=jax.ShapeDtypeStruct((tok, dv), BF16),
        in_specs=[pl.BlockSpec(memory_space=pl.ANY)] * 7,
        out_specs=pl.BlockSpec(memory_space=pltpu.VMEM),
        scratch_shapes=scratch,
        compiler_params=pltpu.CompilerParams(
            collective_id=0, has_side_effects=True, vmem_limit_bytes=60 * 1024 * 1024),
        name="mlstm_layer",
    )(queries, keys, values, input_pre.reshape(1, tok), forget_pre.reshape(1, tok),
      output_pre.reshape(1, tok), w_out)


def solution(mesh, ny=NY):
    nz = mesh.shape["ctx"] // ny
    nx = mesh.shape["head"] // 2
    spec = P("ctx", "head")
    return jax.shard_map(
        functools.partial(local, nz, ny, nx), mesh=mesh, in_specs=(spec,) * 7, out_specs=spec,
        check_vma=False)
```
